256 devices in a mesh: pipe: 16 (over z_hi, y, core), dp: 16 (over x, z_lo).
Axes of the slice: x: 4, y: 4, z: 8 (z_hi: 2, z_lo: 4; z = z_hi * 4 + z_lo), core: 2. Of those that a mesh axis runs over, the one named last changes fastest.
Arguments:
- weights: bfloat16 [16, 2, 7168, 256], P('pipe'), may hold values from -0.375 to 0.375
- gain_model: bfloat16 [16, 7168], P('pipe'), may hold values from 0.099609375 to 1.8984375
- gain_latent: bfloat16 [16, 256], P('pipe'), may hold values from 0.099609375 to 1.8984375
- saved_down: bfloat16 [16, 2, 512, 7168], P('pipe', None, 'dp'), may hold values from -6 to 6
- saved_up: bfloat16 [16, 2, 512, 7168], P('pipe', None, 'dp'), may hold values from -6 to 6
- grad_start: bfloat16 [2, 16, 512, 7168], P(None, 'pipe', 'dp'), may hold values from -0.119628906 to 0.119628906
Outputs:
- section_grads: bfloat16 [16, 2, 7168, 256], P('pipe', None, 'dp')
The draws below stay inside these ranges and needn't reach their ends.
All inputs are finite; a program needn't handle non-finite values.
Results may differ from the reference program's by a relative error of at most 0.024.
Values may be sent and summed in bfloat16 or wider, within the bound.
A program may use at most 128 MiB of HBM per device.

```python
import jax
import jax.numpy as jnp
from jax import lax

D = 7168
LAT = 256
STEPS = 2
SECTIONS = 16
ROWS = 512
N_DP = 16


def block_scale(rng, dims, pieces, least, high):
    def one(axis_at, blocks):
        draws = jax.random.uniform(jax.random.fold_in(jax.random.fold_in(rng, 6), axis_at), (blocks,), jnp.float32, least / len(pieces), high / len(pieces))
        return jnp.repeat(jnp.exp(draws), dims[axis_at] // blocks).reshape((-1,) + (1,) * (len(dims) - axis_at - 1))

    gain = one(*pieces[0])
    for cut in pieces[1:]:
        gain = gain * one(*cut)
    return gain


def centred(key, dims, spread, limit, cuts=(), kind=jnp.bfloat16):
    drawn = spread * jax.random.normal(key, dims, jnp.float32)
    if cuts:
        drawn = drawn * block_scale(key, dims, cuts, -0.22, 0.18)
    return jnp.clip(drawn, -limit, limit).astype(kind)


def setup_inputs(seed: int = 0) -> dict:
    streams_of = jax.random.split(jax.random.key(seed), 7)
    weights = centred(streams_of[0], (SECTIONS, 2, D, LAT), LAT ** -0.5, 0.375, ((0, 16),))
    gain_model = jnp.clip(1.0 + 0.18 * jax.random.normal(streams_of[1], (SECTIONS, D), jnp.float32), 0.099609375, 1.8984375).astype(jnp.bfloat16)
    gain_latent = jnp.clip(1.0 + 0.18 * jax.random.normal(streams_of[2], (SECTIONS, LAT), jnp.float32), 0.099609375, 1.8984375).astype(jnp.bfloat16)
    saved_down = centred(streams_of[3], (SECTIONS, STEPS, ROWS, D), 1.0, 6.0, ((0, 16), (2, 16)))
    saved_up = centred(streams_of[4], (SECTIONS, STEPS, ROWS, D), 1.0, 6.0, ((0, 16), (2, 16)))
    grad_start = centred(streams_of[5], (2, SECTIONS, ROWS, D), 0.02, 0.119628906, ((1, 16), (2, 16)))
    return {"weights": weights, "gain_model": gain_model, "gain_latent": gain_latent, "saved_down": saved_down, "saved_up": saved_up, "grad_start": grad_start}


EPS = 1e-06

def backward(inputs, incoming, pair, gain_in, gain_lat, need_input):
    xf = inputs.astype(jnp.float32)
    inv_in = lax.rsqrt(lax.optimization_barrier(jnp.mean(xf * xf, axis=-1, keepdims=True)) + EPS)
    normed = (xf * inv_in * gain_in.astype(jnp.float32)).astype(jnp.bfloat16)
    latent = jnp.dot(normed, pair[0], preferred_element_type=jnp.float32)
    inv_lat = lax.rsqrt(lax.optimization_barrier(jnp.mean(latent * latent, axis=-1, keepdims=True)) + EPS)
    keyed = (latent * inv_lat * gain_lat.astype(jnp.float32)).astype(jnp.bfloat16)
    dkey = jnp.dot(incoming, pair[1], preferred_element_type=jnp.float32)
    scaled = dkey * gain_lat.astype(jnp.float32)
    dlat = (inv_lat * (scaled - latent * inv_lat * inv_lat * lax.optimization_barrier(jnp.mean(scaled * latent, axis=-1, keepdims=True)))).astype(jnp.bfloat16)
    result = None
    if need_input:
        dnorm = jnp.dot(dlat, pair[0].T, preferred_element_type=jnp.float32)
        vgrad = dnorm * gain_in.astype(jnp.float32)
        result = (incoming.astype(jnp.float32) + inv_in * (vgrad - xf * inv_in * inv_in * lax.optimization_barrier(jnp.mean(vgrad * xf, axis=-1, keepdims=True)))).astype(jnp.bfloat16)
    return (normed, keyed, dlat, result)

def replica_terms(inputs, incoming, pair, gain_in, gain_lat):
    normed, keyed, dlat, unused = backward(inputs, incoming, pair, gain_in, gain_lat, False)
    rows = inputs.shape[0]
    per = rows // N_DP
    normed = normed.reshape(N_DP, per, -1).astype(jnp.float32)
    dlat = dlat.reshape(N_DP, per, -1).astype(jnp.float32)
    keyed = keyed.reshape(N_DP, per, -1).astype(jnp.float32)
    upper = incoming.reshape(N_DP, per, -1).astype(jnp.float32)
    first = jnp.einsum('jti,jtk->jik', normed, dlat)
    second = jnp.einsum('jti,jtk->jik', upper, keyed)
    return jnp.stack([first, second], axis=1)

def reference(weights, gain_model, gain_latent, saved_down, saved_up, grad_start):
    sections = weights.shape[0]
    order = jnp.arange(sections)

    def input_grad(inputs, incoming, section):
        return backward(inputs, incoming, weights[section], gain_model[section], gain_latent[section], True)[3]
    down0 = lax.map(lambda s: input_grad(saved_down[s, 0], grad_start[0, s], s), order)
    up0 = lax.map(lambda r: input_grad(saved_up[r, 0], grad_start[1, r], sections - 1 - r), order)
    zero = jnp.zeros_like(down0[:1])
    down_in = jnp.concatenate([down0[1:], zero], axis=0)
    up_in = jnp.concatenate([zero, up0[:-1]], axis=0)

    def section_grad(s):
        r = sections - 1 - s
        pair = weights[s]
        g_in = gain_model[s]
        g_lat = gain_latent[s]
        down = replica_terms(saved_down[s, 0], grad_start[0, s], pair, g_in, g_lat) + replica_terms(saved_down[s, 1], down_in[s], pair, g_in, g_lat)
        upward = replica_terms(saved_up[r, 0], grad_start[1, r], pair, g_in, g_lat) + replica_terms(saved_up[r, 1], up_in[r], pair, g_in, g_lat)
        down_low = lax.optimization_barrier(down.astype(jnp.bfloat16)).astype(jnp.float32)
        up_low = lax.optimization_barrier(upward.astype(jnp.bfloat16)).astype(jnp.float32)
        total = lax.optimization_barrier(jnp.sum(down_low, axis=0)) + lax.optimization_barrier(jnp.sum(up_low, axis=0))
        return total.astype(jnp.bfloat16)
    return lax.map(section_grad, order)
```

```python
import jax
import jax.numpy as jnp
from jax import lax
from jax.sharding import PartitionSpec as P

EPS = 1e-06


def contract(left, right):
    return lax.dot_general(
        left, right, (((0,), (0,)), ((), ())), preferred_element_type=jnp.float32
    )


def micro(inputs, incoming, pair, gain_in, gain_lat, need_input):
    xf = inputs.astype(jnp.float32)
    inv_in = lax.rsqrt(jnp.mean(xf * xf, axis=-1, keepdims=True) + EPS)
    normed = (xf * inv_in * gain_in.astype(jnp.float32)).astype(jnp.bfloat16)
    latent = jnp.dot(normed, pair[0], preferred_element_type=jnp.float32)
    inv_lat = lax.rsqrt(jnp.mean(latent * latent, axis=-1, keepdims=True) + EPS)
    keyed = (latent * inv_lat * gain_lat.astype(jnp.float32)).astype(jnp.bfloat16)
    dkey = jnp.dot(incoming, pair[1], preferred_element_type=jnp.float32)
    scaled = dkey * gain_lat.astype(jnp.float32)
    dlat = (
        inv_lat
        * (scaled - latent * inv_lat * inv_lat * jnp.mean(scaled * latent, axis=-1, keepdims=True))
    ).astype(jnp.bfloat16)
    result = None
    if need_input:
        dnorm = lax.dot_general(
            dlat, pair[0], (((1,), (1,)), ((), ())), preferred_element_type=jnp.float32
        )
        vgrad = dnorm * gain_in.astype(jnp.float32)
        result = (
            incoming.astype(jnp.float32)
            + inv_in * (vgrad - xf * inv_in * inv_in * jnp.mean(vgrad * xf, axis=-1, keepdims=True))
        ).astype(jnp.bfloat16)
    return result, normed, keyed, dlat


def per_device(weights, gain_model, gain_latent, saved_down, saved_up, grad_start):
    ranks = lax.axis_size("pipe")
    own = weights[0]
    own_in = gain_model[0]
    own_lat = gain_latent[0]
    mirror = [(i, ranks - 1 - i) for i in range(ranks)]
    up_x0 = lax.ppermute(saved_up[0, 0], "pipe", mirror)
    up_y0 = lax.ppermute(grad_start[1, 0], "pipe", mirror)
    up_x1 = lax.ppermute(saved_up[0, 1], "pipe", mirror)
    behind = [(i, i - 1) for i in range(1, ranks)]
    down_y0 = grad_start[0, 0]
    down_z, n_d0, k_d0, q_d0 = micro(saved_down[0, 0], down_y0, own, own_in, own_lat, True)
    down_y1 = lax.ppermute(down_z, "pipe", behind)
    up_z, n_u0, k_u0, q_u0 = micro(up_x0, up_y0, own, own_in, own_lat, True)
    up_y1 = lax.ppermute(up_z, "pipe", behind)
    _, n_d1, k_d1, q_d1 = micro(saved_down[0, 1], down_y1, own, own_in, own_lat, False)
    _, n_u1, k_u1, q_u1 = micro(up_x1, up_y1, own, own_in, own_lat, False)
    n = jnp.concatenate([n_d0, n_u0, n_d1, n_u1], axis=0)
    q = jnp.concatenate([q_d0, q_u0, q_d1, q_u1], axis=0)
    y = jnp.concatenate([down_y0, up_y0, down_y1, up_y1], axis=0)
    k = jnp.concatenate([k_d0, k_u0, k_d1, k_u1], axis=0)
    terms = jnp.stack([contract(n, q), contract(y, k)]).astype(jnp.bfloat16)
    total = lax.psum_scatter(terms, "dp", scatter_dimension=1, tiled=True)
    return total.astype(jnp.bfloat16)[None]


def solution(mesh):
    placed = (
        P("pipe", None, None, None),
        P("pipe", None),
        P("pipe", None),
        P("pipe", None, "dp", None),
        P("pipe", None, "dp", None),
        P(None, "pipe", "dp", None),
    )
    return jax.shard_map(
        per_device,
        mesh=mesh,
        in_specs=placed,
        out_specs=P("pipe", None, "dp", None),
        check_vma=False,
    )
```

```python
import jax
import jax.numpy as jnp
from jax import lax
from jax.experimental import pallas as pl
from jax.experimental.pallas import tpu as pltpu
from jax.sharding import PartitionSpec as P

EPS = 1e-06
MESH = pl.DeviceIdType.MESH
BF = jnp.bfloat16
F32 = jnp.float32
X = 4
Z = 4
CHUNK = 1024


def kernel(w_hbm, sd_hbm, su_hbm, gs_hbm, gm_ref, gl_ref, out_ref,
           w, xr, yr, xg, zr, xq, yq, ak, acc, sb, rb, kept,
           lsem, bsem_s, bsem_r, rsem_s, rsem_r, xs_s, xs_r, zs_s, zs_r):
    pipe = lax.axis_index("pipe")
    dp = lax.axis_index("dp")
    ranks = lax.axis_size("pipe")
    x = dp // Z
    z = lax.rem(dp, Z)
    rows, width = xr.shape[1], xr.shape[2]
    quarter = width // X
    block = quarter // Z
    lat = w.shape[2]
    chunks = width // CHUNK

    loads = []
    for i, (src, dst) in enumerate([
        (sd_hbm.at[0, 0], xr.at[0]), (w_hbm.at[0, 0], w.at[0]), (gs_hbm.at[0, 0], yr.at[0]),
        (w_hbm.at[0, 1], w.at[1]), (sd_hbm.at[0, 1], xr.at[2]),
    ]):
        c = pltpu.make_async_copy(src, dst, lsem.at[i])
        c.start()
        loads.append(c)

    mirror = {"pipe": ranks - 1 - pipe, "dp": x * Z + lax.rem(z + 2, Z)}
    xpeer = [{"pipe": pipe, "dp": lax.rem(x + k, X) * Z + z} for k in range(1, X)]
    zpeer = [{"pipe": pipe, "dp": x * Z + lax.rem(z + k, Z)} for k in range(1, Z)]
    before = {"pipe": lax.rem(pipe + ranks - 1, ranks), "dp": dp}
    after = {"pipe": lax.rem(pipe + 1, ranks), "dp": dp}
    barrier = pltpu.get_barrier_semaphore()
    greet = [mirror, before, after] + xpeer + zpeer
    for d in greet:
        pl.semaphore_signal(barrier, inc=1, device_id=d, device_id_type=MESH)
    pl.semaphore_wait(barrier, len(greet))

    def remote(src, dst, ss, rs, dev):
        return pltpu.make_async_remote_copy(
            src_ref=src, dst_ref=dst, send_sem=ss, recv_sem=rs, device_id=dev, device_id_type=MESH)

    up_x0 = remote(su_hbm.at[0, 0], xr.at[1], bsem_s.at[0], bsem_r.at[0], mirror)
    up_y0 = remote(gs_hbm.at[1, 0], yr.at[1], bsem_s.at[1], bsem_r.at[1], mirror)
    up_x1 = remote(su_hbm.at[0, 1], xr.at[3], bsem_s.at[2], bsem_r.at[2], mirror)
    up_x0.start()
    up_y0.start()

    h = gl_ref[...].astype(F32)
    tokens = pl.ds(pl.multiple_of(x * rows, rows), rows)
    mine = pl.ds(pl.multiple_of(x * quarter, 128), quarter)

    def phase_c(m):
        def body(i, carry):
            ss, total = carry
            cols = pl.ds(pl.multiple_of(i * CHUNK, CHUNK), CHUNK)
            xf = xr[m, :, cols].astype(F32)
            ss = ss + jnp.sum(xf * xf, axis=-1, keepdims=True)
            g = (xf * gm_ref[:, cols].astype(F32)).astype(BF)
            xg[m, :, cols] = g
            total = total + jnp.dot(g, w[0, cols, :], preferred_element_type=F32)
            return ss, total
        ss, total = lax.fori_loop(
            0, chunks, body, (jnp.zeros((rows, 1), F32), jnp.zeros((rows, lat), F32)))
        a = lax.rsqrt(ss / width + EPS)
        c = total * a
        b = lax.rsqrt(jnp.mean(c * c, axis=-1, keepdims=True) + EPS)
        ak[m, tokens, pl.ds(lat, lat)] = (c * b * h).astype(BF)
        return a, b, c, total

    def phase_e(m, state):
        a, b, c, total = state
        def body(i, e):
            cols = pl.ds(pl.multiple_of(i * CHUNK, CHUNK), CHUNK)
            return e + jnp.dot(yr[m, :, cols], w[1, cols, :], preferred_element_type=F32)
        e = lax.fori_loop(0, chunks, body, jnp.zeros((rows, lat), F32))
        u = e * h
        q = b * (u - c * b * b * jnp.mean(u * c, axis=-1, keepdims=True))
        ak[m, tokens, pl.ds(0, lat)] = (a * q).astype(BF)
        return q.astype(BF)

    def phase_z(m, slot, state, q):
        a, b, c, total = state
        mean = jnp.sum(total * q.astype(F32), axis=-1, keepdims=True) / width
        scale = a * a * mean
        def body(i, carry):
            cols = pl.ds(pl.multiple_of(i * CHUNK, CHUNK), CHUNK)
            v = lax.dot_general(q, w[0, cols, :], (((1,), (1,)), ((), ())), preferred_element_type=F32)
            v = v * gm_ref[:, cols].astype(F32)
            zz = yr[m, :, cols].astype(F32) + a * (v - xr[m, :, cols].astype(F32) * scale)
            zr[slot, :, cols] = zz.astype(BF)
            return carry
        lax.fori_loop(0, chunks, body, 0)

    pending = []

    def spread(what, m):
        out = []
        for k in range(1, X):
            far = pl.ds(pl.multiple_of(lax.rem(x + k, X) * quarter, 128), quarter)
            if what == 0:
                src, dst = xg.at[m, :, far], xq.at[m, tokens, :]
            elif what == 1:
                src, dst = yr.at[m, :, far], yq.at[m, tokens, :]
            else:
                src, dst = ak.at[m, tokens, :], ak.at[m, tokens, :]
            c = remote(src, dst, xs_s.at[what, m, k - 1], xs_r.at[what, m, k - 1], xpeer[k - 1])
            c.start()
            out.append(c)
        if what == 0:
            xq[m, tokens, :] = xg[m, :, mine]
        elif what == 1:
            yq[m, tokens, :] = yr[m, :, mine]
        pending.append((m, out))

    def relay(slot, m):
        return remote(zr.at[slot], yr.at[m], rsem_s.at[slot], rsem_r.at[slot], before)

    def gather(m):
        for mm, cs in pending:
            if mm == m:
                for c in cs:
                    c.wait_recv()

    def grads(m, first):
        def body(i, carry):
            cols = pl.ds(pl.multiple_of(i * 256, 256), 256)
            for half, src in ((0, xq), (1, yq)):
                t = lax.dot_general(src[m, :, cols], ak[m, :, pl.ds(half * lat, lat)],
                                    (((0,), (0,)), ((), ())), preferred_element_type=F32)
                if first:
                    acc[half, cols, :] = t
                else:
                    acc[half, cols, :] += t
            return carry
        lax.fori_loop(0, quarter // 256, body, 0)

    loads[0].wait()
    loads[1].wait()
    s0 = phase_c(0)
    spread(0, 0)
    loads[2].wait()
    loads[3].wait()
    spread(1, 0)
    q0 = phase_e(0, s0)
    spread(2, 0)
    phase_z(0, 0, s0, q0)
    down = relay(0, 2)

    @pl.when(pipe > 0)
    def _():
        down.start()

    loads[4].wait()
    s2 = phase_c(2)
    spread(0, 2)

    up_x0.wait_send()
    up_y0.wait_send()
    up_x1.start()
    up_x0.wait_recv()
    s1 = phase_c(1)
    up_y0.wait_recv()
    q1 = phase_e(1, s1)
    phase_z(1, 1, s1, q1)
    up = relay(1, 3)

    @pl.when(pipe > 0)
    def _():
        up.start()

    spread(0, 1)
    spread(1, 1)
    spread(2, 1)
    gather(0)
    grads(0, True)

    @pl.when(pipe < ranks - 1)
    def _():
        down.wait_recv()

    @pl.when(pipe == ranks - 1)
    def _():
        yr[2] = jnp.zeros((rows, width), BF)
        yr[3] = jnp.zeros((rows, width), BF)

    spread(1, 2)
    phase_e(2, s2)
    spread(2, 2)
    up_x1.wait_recv()
    s3 = phase_c(3)
    spread(0, 3)
    gather(1)
    grads(1, False)
    gather(2)
    grads(2, False)

    @pl.when(pipe < ranks - 1)
    def _():
        up.wait_recv()

    spread(1, 3)
    phase_e(3, s3)
    spread(2, 3)
    gather(3)
    grads(3, False)

    sends = []
    for k in (2, 1, 3):
        far = pl.ds(pl.multiple_of(lax.rem(z + k, Z) * block, 16), block)
        sb[k - 1] = acc[:, far, :].astype(BF)
        c = remote(sb.at[k - 1], rb.at[k - 1], zs_s.at[k - 1], zs_r.at[k - 1], zpeer[k - 1])
        c.start()
        sends.append(c)
    near = pl.ds(pl.multiple_of(z * block, 16), block)
    total = acc[:, near, :].astype(BF).astype(F32)
    for c in sends:
        c.wait_recv()
    for k in range(1, Z):
        total = total + rb[k - 1].astype(F32)
    out_ref[...] = total.astype(BF)

    for c in sends:
        c.wait_send()
    for mm, cs in pending:
        for c in cs:
            c.wait_send()
    up_x1.wait_send()

    @pl.when(pipe > 0)
    def _():
        down.wait_send()
        up.wait_send()


def per_device(weights, gain_model, gain_latent, saved_down, saved_up, grad_start):
    _, _, width, lat = weights.shape
    rows = saved_down.shape[2]
    quarter = width // X
    block = quarter // Z
    dma = pltpu.SemaphoreType.DMA
    any_spec = pl.BlockSpec(memory_space=pl.ANY)
    vmem = pl.BlockSpec(memory_space=pltpu.VMEM)
    out = pl.pallas_call(
        kernel,
        out_shape=jax.ShapeDtypeStruct((2, block, lat), BF),
        in_specs=[any_spec] * 4 + [vmem] * 2,
        out_specs=vmem,
        scratch_shapes=[
            pltpu.VMEM((2, width, lat), BF),
            pltpu.VMEM((4, rows, width), BF),
            pltpu.VMEM((4, rows, width), BF),
            pltpu.VMEM((4, rows, width), BF),
            pltpu.VMEM((2, rows, width), BF),
            pltpu.VMEM((4, X * rows, quarter), BF),
            pltpu.VMEM((4, X * rows, quarter), BF),
            pltpu.VMEM((4, X * rows, 2 * lat), BF),
            pltpu.VMEM((2, quarter, lat), F32),
            pltpu.VMEM((3, 2, block, lat), BF),
            pltpu.VMEM((3, 2, block, lat), BF),
            pltpu.VMEM((8, 128), F32),
            dma((5,)),
            dma((3,)), dma((3,)),
            dma((2,)), dma((2,)),
            dma((3, 4, 3)), dma((3, 4, 3)),
            dma((3,)), dma((3,)),
        ],
        compiler_params=pltpu.CompilerParams(
            collective_id=0, has_side_effects=True, vmem_limit_bytes=56 << 20),
        name="relay_step",
    )(weights, saved_down, saved_up, grad_start, gain_model, gain_latent)
    return out[None]


def solution(mesh):
    placed = (
        P("pipe", None, None, None),
        P("pipe", None),
        P("pipe", None),
        P("pipe", None, "dp", None),
        P("pipe", None, "dp", None),
        P(None, "pipe", "dp", None),
    )
    return jax.shard_map(
        per_device,
        mesh=mesh,
        in_specs=placed,
        out_specs=P("pipe", None, "dp", None),
        check_vma=False,
    )
```

```python
import jax
import jax.numpy as jnp
from jax import lax
from jax.experimental import pallas as pl
from jax.experimental.pallas import tpu as pltpu
from jax.sharding import PartitionSpec as P

EPS = 1e-06
MESH = pl.DeviceIdType.MESH
BF = jnp.bfloat16
F32 = jnp.float32
X = 4
Z = 4
STEP = 1792
UX0, UY0, DX0, DY0, UX1, DX1 = range(6)


def kernel(w_hbm, sd_hbm, su_hbm, gs_hbm, gm_ref, gl_ref, out_ref,
           raw, w, xs, xg, ys, zr, inv, pf, pb, pr, kk, qq, acc, sb, rb, via,
           lsem, in_s, in_r, a_s, a_r, rs_s, rs_r, ag_s, ag_r, rl_s, rl_r, gr_s, gr_r, via_s, via_r):
    pipe = lax.axis_index("pipe")
    dp = lax.axis_index("dp")
    ranks = lax.axis_size("pipe")
    x = dp // Z
    z = lax.rem(dp, Z)
    rows, width = raw.shape[1], raw.shape[2]
    quarter = width // X
    block = quarter // Z
    lat = w.shape[2]
    tokens = X * rows

    inputs = [su_hbm.at[0, 0], gs_hbm.at[1, 0], sd_hbm.at[0, 0], gs_hbm.at[0, 0], su_hbm.at[0, 1], sd_hbm.at[0, 1]]
    mine = pl.ds(pl.multiple_of(x * quarter, 128), quarter)
    here = pl.ds(pl.multiple_of(x * rows, rows), rows)
    raw_loads = {}
    for j, i in enumerate((UX0, DX0, UX1, DX1)):
        raw_loads[i] = (j, pltpu.make_async_copy(inputs[i], raw.at[j], lsem.at[j]))
    own_loads = {}
    for j, (i, dst) in enumerate(((DX0, xs.at[0]), (DY0, ys.at[0]), (DX1, xs.at[2]))):
        own_loads[i] = pltpu.make_async_copy(inputs[i].at[:, mine], dst.at[here], lsem.at[4 + j])
    w_loads = [pltpu.make_async_copy(w_hbm.at[0, half, mine, :], w.at[half], lsem.at[7 + half]) for half in range(2)]
    for c in [raw_loads[UX0][1], own_loads[DX0], w_loads[0], own_loads[DY0], w_loads[1],
              raw_loads[DX0][1], raw_loads[UX1][1], raw_loads[DX1][1], own_loads[DX1]]:
        c.start()

    mirror = [{"pipe": ranks - 1 - pipe, "dp": lax.rem(x + k, X) * Z + lax.rem(z + 2, Z)} for k in range(X)]
    xpeer = [{"pipe": pipe, "dp": lax.rem(x + k, X) * Z + z} for k in range(1, X)]
    zpeer = [{"pipe": pipe, "dp": x * Z + lax.rem(z + k, Z)} for k in range(1, Z)]
    before = {"pipe": lax.rem(pipe + ranks - 1, ranks), "dp": dp}
    after = {"pipe": lax.rem(pipe + 1, ranks), "dp": dp}
    barrier = pltpu.get_barrier_semaphore()
    greet = mirror + [before, after] + xpeer + zpeer
    for d in greet:
        pl.semaphore_signal(barrier, inc=1, device_id=d, device_id_type=MESH)

    def remote(src, dst, ss, rs, dev):
        return pltpu.make_async_remote_copy(
            src_ref=src, dst_ref=dst, send_sem=ss, recv_sem=rs, device_id=dev, device_id_type=MESH)

    def inverse(i):
        j, load = raw_loads[i]
        load.wait()

        def body(n, ss):
            xf = raw[j, :, pl.ds(pl.multiple_of(n * 1024, 1024), 1024)].astype(F32)
            return ss + jnp.sum(xf * xf, axis=-1, keepdims=True)
        ss = lax.fori_loop(0, width // 1024, body, jnp.zeros((rows, 1), F32))
        return jnp.broadcast_to(lax.rsqrt(ss / width + EPS), (rows, 128))

    sent = []

    def cut(i, k):
        return inputs[i].at[:, pl.ds(pl.multiple_of(lax.rem(x + k, X) * quarter, 128), quarter)]

    def send_up(i, dst):
        cs = []
        for k in range(X):
            c = remote(cut(i, k), dst.at[here], in_s.at[i, k], in_r.at[i, k], mirror[k])
            c.start()
            cs.append(c)
        return cs

    def send_down(i, dst):
        cs = []
        for k in range(1, X):
            c = remote(cut(i, k), dst.at[here], in_s.at[i, k], in_r.at[i, k], xpeer[k - 1])
            c.start()
            cs.append(c)
        sent.extend(cs)
        return cs

    pl.semaphore_wait(barrier, len(greet))
    up_x0 = send_up(UX0, xs.at[1])
    up_y0 = send_up(UY0, ys.at[1])
    down_x0 = send_down(DX0, xs.at[0])
    down_y0 = send_down(DY0, ys.at[0])
    down_x1 = send_down(DX1, xs.at[2])
    inv[4] = inverse(UX0)
    up_a0 = remote(inv.at[4], inv.at[1], a_s.at[0], a_r.at[0], mirror[0])
    up_a0.start()
    inv[0] = inverse(DX0)
    h = gl_ref[...].astype(F32)

    def arrive(cs):
        for c in cs:
            c.wait_recv()

    def reduce_start(m, which, part):
        pf[m, which] = part
        pb[m, which] = part.astype(BF)
        cs = []
        for k in range(1, Z):
            far = pl.ds(pl.multiple_of(lax.rem(x + k, X) * rows, rows), rows)
            c = remote(pb.at[m, which, far, :], pr.at[m, which, k - 1],
                       rs_s.at[m, which, k - 1], rs_r.at[m, which, k - 1], xpeer[k - 1])
            c.start()
            cs.append(c)
        sent.extend(cs)
        return cs

    def reduce_end(m, which, cs):
        arrive(cs)
        total = pf[m, which, here, :]
        for k in range(1, Z):
            total = total + pr[m, which, k - 1].astype(F32)
        return total

    def gather_start(m, which, buf):
        cs = []
        for k in range(1, Z):
            c = remote(buf.at[m, here, :], buf.at[m, here, :],
                       ag_s.at[m, which, k - 1], ag_r.at[m, which, k - 1], xpeer[k - 1])
            c.start()
            cs.append(c)
        sent.extend(cs)
        return cs

    def gain(i):
        return gm_ref[:, pl.ds(pl.multiple_of(x * quarter + i * STEP, 128), STEP)].astype(F32)

    def part_c(m):
        def body(i, total):
            cols = pl.ds(pl.multiple_of(i * STEP, STEP), STEP)
            g = (xs[m, :, cols].astype(F32) * gain(i)).astype(BF)
            xg[m, :, cols] = g
            return total + jnp.dot(g, w[0, cols, :], preferred_element_type=F32)
        part = lax.fori_loop(0, quarter // STEP, body, jnp.zeros((tokens, lat), F32))
        return reduce_start(m, 0, part)

    def part_e(m):
        def body(i, total):
            cols = pl.ds(pl.multiple_of(i * STEP, STEP), STEP)
            return total + jnp.dot(ys[m, :, cols], w[1, cols, :], preferred_element_type=F32)
        part = lax.fori_loop(0, quarter // STEP, body, jnp.zeros((tokens, lat), F32))
        return reduce_start(m, 1, part)

    def latent_k(m, cs):
        total = reduce_end(m, 0, cs)
        a = inv[m, :, 0:1]
        c = total * a
        b = lax.rsqrt(jnp.mean(c * c, axis=-1, keepdims=True) + EPS)
        kk[m, here, :] = (c * b * h).astype(BF)
        return (a, b, c, total), gather_start(m, 0, kk)

    def latent_q(m, state, cs):
        a, b, c, total = state
        u = reduce_end(m, 1, cs) * h
        q = b * (u - c * b * b * jnp.mean(u * c, axis=-1, keepdims=True))
        aq = (a * q).astype(BF)
        t = a * a * jnp.sum(total * aq.astype(F32), axis=-1, keepdims=True) / width
        qq[m, here, 0:lat] = aq
        qq[m, here, lat:lat + 128] = jnp.broadcast_to(t, (rows, 128)).astype(BF)
        return gather_start(m, 1, qq)

    def input_grad(m):
        q = qq[m, :, 0:lat]
        t = qq[m, :, lat:lat + 1].astype(F32)
        def body(i, carry):
            cols = pl.ds(pl.multiple_of(i * STEP, STEP), STEP)
            v = lax.dot_general(q, w[0, cols, :], (((1,), (1,)), ((), ())), preferred_element_type=F32)
            zz = ys[m, :, cols].astype(F32) + v * gain(i) - xs[m, :, cols].astype(F32) * t
            zr[m, :, cols] = zz.astype(BF)
            return carry
        lax.fori_loop(0, quarter // STEP, body, 0)

    def relay(m):
        return remote(zr.at[m], ys.at[m + 2], rl_s.at[m], rl_r.at[m], before)

    def grads(half, m):
        def body(i, carry):
            cols = pl.ds(pl.multiple_of(i * STEP, STEP), STEP)
            left = xg[m, :, cols] if half == 0 else ys[m, :, cols]
            right = qq[m, :, 0:lat] if half == 0 else kk[m]
            t = lax.dot_general(left, right, (((0,), (0,)), ((), ())), preferred_element_type=F32)
            if m == 0:
                acc[half, cols, :] = t
            else:
                acc[half, cols, :] += t
            return carry
        lax.fori_loop(0, quarter // STEP, body, 0)

    def far_block(k):
        return pl.ds(pl.multiple_of(lax.rem(z + k, Z) * block, 16), block)

    inner = jnp.logical_or(z == 1, z == 2)
    direct = [[remote(sb.at[half, k - 1], rb.at[half, k - 1], gr_s.at[half, k - 1], gr_r.at[half, k - 1], zpeer[k - 1])
               for k in range(1, Z)] for half in range(2)]
    ahead = [{k - 1: remote(sb.at[half, k - 1], via.at[half], via_s.at[half], via_r.at[half], zpeer[Z - k - 1])
              for k in (1, 3)} for half in range(2)]

    def blocks_start(half):
        @pl.when(z == 0)
        def _():
            for k in (3, 2, 1):
                sb[half, k - 1] = acc[half, far_block(k), :].astype(BF)
                (ahead if k == 3 else direct)[half][k - 1].start()

        @pl.when(z == 3)
        def _():
            for k in (1, 2, 3):
                sb[half, k - 1] = acc[half, far_block(k), :].astype(BF)
                (ahead if k == 1 else direct)[half][k - 1].start()

        @pl.when(inner)
        def _():
            for k in (1, 3):
                sb[half, k - 1] = acc[half, far_block(k), :].astype(BF)
                direct[half][k - 1].start()

    def blocks_pass(half):
        @pl.when(inner)
        def _():
            ahead[half][0].wait_recv()
            sb[half, 1] = (acc[half, far_block(2), :] + via[half].astype(F32)).astype(BF)
            direct[half][1].start()

    def blocks_end(half):
        near = pl.ds(pl.multiple_of(z * block, 16), block)
        total = acc[half, near, :].astype(BF).astype(F32)
        direct[half][1].wait_recv()
        total = total + rb[half, 1].astype(F32)

        @pl.when(z == 0)
        def _():
            direct[half][2].wait_recv()
            out_ref[half] = (total + rb[half, 2].astype(F32)).astype(BF)

        @pl.when(z == 3)
        def _():
            direct[half][0].wait_recv()
            out_ref[half] = (total + rb[half, 0].astype(F32)).astype(BF)

        @pl.when(inner)
        def _():
            direct[half][0].wait_recv()
            direct[half][2].wait_recv()
            out_ref[half] = (total + rb[half, 0].astype(F32) + rb[half, 2].astype(F32)).astype(BF)

    def blocks_sent(half):
        direct[half][1].wait_send()

        @pl.when(z == 0)
        def _():
            ahead[half][2].wait_send()
            direct[half][0].wait_send()

        @pl.when(z == 3)
        def _():
            ahead[half][0].wait_send()
            direct[half][2].wait_send()

        @pl.when(inner)
        def _():
            direct[half][0].wait_send()
            direct[half][2].wait_send()

    for i in (DX0, DY0):
        own_loads[i].wait()
    for c in w_loads:
        c.wait()
    arrive(down_x0)
    rc0 = part_c(0)
    arrive(down_y0)
    re0 = part_e(0)
    s0, gk0 = latent_k(0, rc0)
    gq0 = latent_q(0, s0, re0)
    arrive(gq0)
    input_grad(0)
    down = relay(0)

    @pl.when(pipe > 0)
    def _():
        down.start()

    inv[5] = inverse(UX1)
    inv[2] = inverse(DX1)
    arrive(gk0)
    grads(0, 0)
    grads(1, 0)
    own_loads[DX1].wait()
    arrive(down_x1)
    rc2 = part_c(2)
    s2, gk2 = latent_k(2, rc2)

    for c in up_x0 + up_y0:
        c.wait_send()
    up_x1 = send_up(UX1, xs.at[3])
    up_a1 = remote(inv.at[5], inv.at[3], a_s.at[1], a_r.at[1], mirror[0])
    up_a1.start()
    arrive(up_x0)
    rc1 = part_c(1)
    arrive(up_y0)
    re1 = part_e(1)
    up_a0.wait_recv()
    s1, gk1 = latent_k(1, rc1)
    gq1 = latent_q(1, s1, re1)
    arrive(gq1)
    input_grad(1)
    up = relay(1)

    @pl.when(pipe > 0)
    def _():
        up.start()

    @pl.when(pipe < ranks - 1)
    def _():
        down.wait_recv()

    @pl.when(pipe == ranks - 1)
    def _():
        ys[2] = jnp.zeros((tokens, quarter), BF)
        ys[3] = jnp.zeros((tokens, quarter), BF)

    re2 = part_e(2)
    arrive(gk1)
    grads(0, 1)
    grads(1, 1)
    gq2 = latent_q(2, s2, re2)
    arrive(gk2)
    grads(1, 2)
    arrive(gq2)
    grads(0, 2)

    arrive(up_x1)
    rc3 = part_c(3)

    @pl.when(pipe < ranks - 1)
    def _():
        up.wait_recv()

    re3 = part_e(3)
    up_a1.wait_recv()
    s3, gk3 = latent_k(3, rc3)
    gq3 = latent_q(3, s3, re3)
    arrive(gk3)
    grads(1, 3)
    blocks_start(1)
    arrive(gq3)
    grads(0, 3)
    blocks_pass(1)
    blocks_start(0)
    blocks_pass(0)
    blocks_end(1)
    blocks_end(0)
    blocks_sent(1)
    blocks_sent(0)

    for c in sent + up_x1 + [up_a0, up_a1]:
        c.wait_send()

    @pl.when(pipe > 0)
    def _():
        down.wait_send()
        up.wait_send()


def per_device(weights, gain_model, gain_latent, saved_down, saved_up, grad_start):
    _, _, width, lat = weights.shape
    rows = saved_down.shape[2]
    quarter = width // X
    block = quarter // Z
    tokens = X * rows
    dma = pltpu.SemaphoreType.DMA
    any_spec = pl.BlockSpec(memory_space=pl.ANY)
    vmem = pl.BlockSpec(memory_space=pltpu.VMEM)
    out = pl.pallas_call(
        kernel,
        out_shape=jax.ShapeDtypeStruct((2, block, lat), BF),
        in_specs=[any_spec] * 4 + [vmem] * 2,
        out_specs=vmem,
        scratch_shapes=[
            pltpu.VMEM((4, rows, width), BF),
            pltpu.VMEM((2, quarter, lat), BF),
            pltpu.VMEM((4, tokens, quarter), BF),
            pltpu.VMEM((4, tokens, quarter), BF),
            pltpu.VMEM((4, tokens, quarter), BF),
            pltpu.VMEM((2, tokens, quarter), BF),
            pltpu.VMEM((6, rows, 128), F32),
            pltpu.VMEM((4, 2, tokens, lat), F32),
            pltpu.VMEM((4, 2, tokens, lat), BF),
            pltpu.VMEM((4, 2, 3, rows, lat), BF),
            pltpu.VMEM((4, tokens, lat), BF),
            pltpu.VMEM((4, tokens, lat + 128), BF),
            pltpu.VMEM((2, quarter, lat), F32),
            pltpu.VMEM((2, 3, block, lat), BF),
            pltpu.VMEM((2, 3, block, lat), BF),
            pltpu.VMEM((2, block, lat), BF),
            dma((9,)),
            dma((6, 4)), dma((6, 4)),
            dma((2,)), dma((2,)),
            dma((4, 2, 3)), dma((4, 2, 3)),
            dma((4, 2, 3)), dma((4, 2, 3)),
            dma((2,)), dma((2,)),
            dma((2, 3)), dma((2, 3)),
            dma((2,)), dma((2,)),
        ],
        compiler_params=pltpu.CompilerParams(
            collective_id=0, has_side_effects=True, vmem_limit_bytes=56 << 20),
        name="relay_step",
    )(weights, saved_down, saved_up, grad_start, gain_model, gain_latent)
    return out[None]


def solution(mesh):
    placed = (
        P("pipe", None, None, None),
        P("pipe", None),
        P("pipe", None),
        P("pipe", None, "dp", None),
        P("pipe", None, "dp", None),
        P(None, "pipe", "dp", None),
    )
    return jax.shard_map(
        per_device,
        mesh=mesh,
        in_specs=placed,
        out_specs=P("pipe", None, "dp", None),
        check_vma=False,
    )
```

```python
import jax
import jax.numpy as jnp
from jax import lax
from jax.experimental import pallas as pl
from jax.experimental.pallas import tpu as pltpu
from jax.sharding import PartitionSpec as P

EPS = 1e-06
MESH = pl.DeviceIdType.MESH
BF = jnp.bfloat16
F32 = jnp.float32
X = 4
Z = 4
STEP = 1792
UX0, UY0, DX0, DY0, UX1, DX1 = range(6)


def kernel(w_hbm, sd_hbm, su_hbm, gs_hbm, gm_ref, gl_ref, out_ref,
           raw, w, xs, xg, ys, zr, inv, pf, pb, pr, kk, qq, acc, sb, rb, via, fw,
           lsem, in_s, in_r, a_s, a_r, rs_s, rs_r, ag_s, ag_r, rl_s, rl_r, gr_s, gr_r, via_s, via_r, fs_s, fs_r, ff_s, ff_r):
    pipe = lax.axis_index("pipe")
    dp = lax.axis_index("dp")
    ranks = lax.axis_size("pipe")
    x = dp // Z
    z = lax.rem(dp, Z)
    rows, width = raw.shape[1], raw.shape[2]
    quarter = width // X
    block = quarter // Z
    lat = w.shape[2]
    tokens = X * rows

    inputs = [su_hbm.at[0, 0], gs_hbm.at[1, 0], sd_hbm.at[0, 0], gs_hbm.at[0, 0], su_hbm.at[0, 1], sd_hbm.at[0, 1]]
    mine = pl.ds(pl.multiple_of(x * quarter, 128), quarter)
    here = pl.ds(pl.multiple_of(x * rows, rows), rows)
    raw_loads = {}
    for j, i in enumerate((UX0, DX0, UX1, DX1)):
        raw_loads[i] = (j, pltpu.make_async_copy(inputs[i], raw.at[j], lsem.at[j]))
    own_loads = {}
    for j, (i, dst) in enumerate(((DX0, xs.at[0]), (DY0, ys.at[0]), (DX1, xs.at[2]))):
        own_loads[i] = pltpu.make_async_copy(inputs[i].at[:, mine], dst.at[here], lsem.at[4 + j])
    w_loads = [pltpu.make_async_copy(w_hbm.at[0, half, mine, :], w.at[half], lsem.at[7 + half]) for half in range(2)]
    for c in [raw_loads[UX0][1], own_loads[DX0], w_loads[0], own_loads[DY0], w_loads[1],
              raw_loads[DX0][1], raw_loads[UX1][1], raw_loads[DX1][1], own_loads[DX1]]:
        c.start()

    mirror = [{"pipe": ranks - 1 - pipe, "dp": lax.rem(x + k, X) * Z + lax.rem(z + 2, Z)} for k in range(X)]
    xpeer = [{"pipe": pipe, "dp": lax.rem(x + k, X) * Z + z} for k in range(1, X)]
    zpeer = [{"pipe": pipe, "dp": x * Z + lax.rem(z + k, Z)} for k in range(1, Z)]
    before = {"pipe": lax.rem(pipe + ranks - 1, ranks), "dp": dp}
    after = {"pipe": lax.rem(pipe + 1, ranks), "dp": dp}
    barrier = pltpu.get_barrier_semaphore()
    greet = mirror + [before, after] + xpeer + zpeer
    for d in greet:
        pl.semaphore_signal(barrier, inc=1, device_id=d, device_id_type=MESH)

    edge = ranks // 2
    is_edge = pipe == edge
    is_end = pipe == edge - 1
    stops = [{"pipe": edge + 2 * j, "dp": dp} for j in range(1, X)]
    is_stop = jnp.logical_or(pipe == edge + 2, jnp.logical_or(pipe == edge + 4, pipe == edge + 6))
    ends = {"pipe": edge - 1, "dp": dp}

    @pl.when(jnp.logical_or(is_edge, is_end))
    def _():
        for d in stops:
            pl.semaphore_signal(barrier, inc=1, device_id=d, device_id_type=MESH)

    @pl.when(is_stop)
    def _():
        for d in ({"pipe": edge, "dp": dp}, ends):
            pl.semaphore_signal(barrier, inc=1, device_id=d, device_id_type=MESH)

    def remote(src, dst, ss, rs, dev):
        return pltpu.make_async_remote_copy(
            src_ref=src, dst_ref=dst, send_sem=ss, recv_sem=rs, device_id=dev, device_id_type=MESH)

    def inverse(i):
        j, load = raw_loads[i]
        load.wait()

        def body(n, ss):
            xf = raw[j, :, pl.ds(pl.multiple_of(n * 1024, 1024), 1024)].astype(F32)
            return ss + jnp.sum(xf * xf, axis=-1, keepdims=True)
        ss = lax.fori_loop(0, width // 1024, body, jnp.zeros((rows, 1), F32))
        return jnp.broadcast_to(lax.rsqrt(ss / width + EPS), (rows, 128))

    sent = []

    def cut(i, k):
        return inputs[i].at[:, pl.ds(pl.multiple_of(lax.rem(x + k, X) * quarter, 128), quarter)]

    def send_up(i, dst):
        cs = []
        for k in range(X):
            c = remote(cut(i, k), dst.at[here], in_s.at[i, k], in_r.at[i, k], mirror[k])
            c.start()
            cs.append(c)
        return cs

    def send_down(i, dst):
        cs = []
        for k in range(1, X):
            c = remote(cut(i, k), dst.at[here], in_s.at[i, k], in_r.at[i, k], xpeer[k - 1])
            c.start()
            cs.append(c)
        sent.extend(cs)
        return cs

    turn = jnp.logical_or(is_edge, is_end)

    @pl.when(turn)
    def _():
        pl.semaphore_wait(barrier, len(greet) + len(stops))

    @pl.when(is_stop)
    def _():
        pl.semaphore_wait(barrier, len(greet) + 2)

    @pl.when(jnp.logical_not(jnp.logical_or(turn, is_stop)))
    def _():
        pl.semaphore_wait(barrier, len(greet))

    up_x0 = send_up(UX0, xs.at[1])
    up_y0 = send_up(UY0, ys.at[1])
    down_x0 = send_down(DX0, xs.at[0])
    down_y0 = send_down(DY0, ys.at[0])
    down_x1 = send_down(DX1, xs.at[2])
    inv[4] = inverse(UX0)
    up_a0 = remote(inv.at[4], inv.at[1], a_s.at[0], a_r.at[0], mirror[0])
    up_a0.start()
    inv[0] = inverse(DX0)
    h = gl_ref[...].astype(F32)

    def arrive(cs):
        for c in cs:
            c.wait_recv()

    def reduce_start(m, which, part):
        pf[m, which] = part
        pb[m, which] = part.astype(BF)
        cs = []
        for k in range(1, Z):
            far = pl.ds(pl.multiple_of(lax.rem(x + k, X) * rows, rows), rows)
            c = remote(pb.at[m, which, far, :], pr.at[m, which, k - 1],
                       rs_s.at[m, which, k - 1], rs_r.at[m, which, k - 1], xpeer[k - 1])
            c.start()
            cs.append(c)
        sent.extend(cs)
        return cs

    def reduce_end(m, which, cs):
        arrive(cs)
        total = pf[m, which, here, :]
        for k in range(1, Z):
            total = total + pr[m, which, k - 1].astype(F32)
        return total

    def gather_start(m, which, buf):
        cs = []
        for k in range(1, Z):
            c = remote(buf.at[m, here, :], buf.at[m, here, :],
                       ag_s.at[m, which, k - 1], ag_r.at[m, which, k - 1], xpeer[k - 1])
            c.start()
            cs.append(c)
        sent.extend(cs)
        return cs

    def gain(i):
        return gm_ref[:, pl.ds(pl.multiple_of(x * quarter + i * STEP, 128), STEP)].astype(F32)

    def part_c(m):
        def body(i, total):
            cols = pl.ds(pl.multiple_of(i * STEP, STEP), STEP)
            g = (xs[m, :, cols].astype(F32) * gain(i)).astype(BF)
            xg[m, :, cols] = g
            return total + jnp.dot(g, w[0, cols, :], preferred_element_type=F32)
        part = lax.fori_loop(0, quarter // STEP, body, jnp.zeros((tokens, lat), F32))
        return reduce_start(m, 0, part)

    def part_e(m):
        def body(i, total):
            cols = pl.ds(pl.multiple_of(i * STEP, STEP), STEP)
            return total + jnp.dot(ys[m, :, cols], w[1, cols, :], preferred_element_type=F32)
        part = lax.fori_loop(0, quarter // STEP, body, jnp.zeros((tokens, lat), F32))
        return reduce_start(m, 1, part)

    def latent_k(m, cs):
        total = reduce_end(m, 0, cs)
        a = inv[m, :, 0:1]
        c = total * a
        b = lax.rsqrt(jnp.mean(c * c, axis=-1, keepdims=True) + EPS)
        kk[m, here, :] = (c * b * h).astype(BF)
        return (a, b, c, total), gather_start(m, 0, kk)

    def latent_q(m, state, cs):
        a, b, c, total = state
        u = reduce_end(m, 1, cs) * h
        q = b * (u - c * b * b * jnp.mean(u * c, axis=-1, keepdims=True))
        aq = (a * q).astype(BF)
        t = a * a * jnp.sum(total * aq.astype(F32), axis=-1, keepdims=True) / width
        qq[m, here, 0:lat] = aq
        qq[m, here, lat:lat + 128] = jnp.broadcast_to(t, (rows, 128)).astype(BF)
        return gather_start(m, 1, qq)

    def input_grad(m):
        q = qq[m, :, 0:lat]
        t = qq[m, :, lat:lat + 1].astype(F32)
        def body(i, carry):
            cols = pl.ds(pl.multiple_of(i * STEP, STEP), STEP)
            v = lax.dot_general(q, w[0, cols, :], (((1,), (1,)), ((), ())), preferred_element_type=F32)
            zz = ys[m, :, cols].astype(F32) + v * gain(i) - xs[m, :, cols].astype(F32) * t
            zr[m, :, cols] = zz.astype(BF)
            return carry
        lax.fori_loop(0, quarter // STEP, body, 0)

    def relay(m):
        return remote(zr.at[m], ys.at[m + 2], rl_s.at[m], rl_r.at[m], before)

    def relay_parts(m):
        first = pl.ds(0, rows)
        cs = [remote(zr.at[m, first, :], ys.at[m + 2, first, :], rl_s.at[m], rl_r.at[m], before)]
        for j in range(1, X):
            cs.append(remote(zr.at[m, pl.ds(j * rows, rows), :], fw.at[m], fs_s.at[m, j - 1], fs_r.at[m], stops[j - 1]))
        return cs

    def relay_on(m):
        j = (pipe - edge) // 2
        there = pl.ds(pl.multiple_of(j * rows, rows), rows)
        return remote(fw.at[m], ys.at[m + 2, there, :], ff_s.at[m], ff_r.at[m, j - 1], ends)

    def relay_start(m):
        @pl.when(jnp.logical_and(pipe > 0, jnp.logical_not(is_edge)))
        def _():
            relay(m).start()

        @pl.when(is_edge)
        def _():
            for c in relay_parts(m):
                c.start()

    def relay_pass(m):
        @pl.when(is_stop)
        def _():
            remote(zr.at[m, pl.ds(0, rows), :], fw.at[m], fs_s.at[m, 0], fs_r.at[m], stops[0]).wait_recv()
            relay_on(m).start()

    def relay_end(m):
        @pl.when(jnp.logical_and(pipe < ranks - 1, jnp.logical_not(is_end)))
        def _():
            relay(m).wait_recv()

        @pl.when(is_end)
        def _():
            first = pl.ds(0, rows)
            remote(zr.at[m, first, :], ys.at[m + 2, first, :], rl_s.at[m], rl_r.at[m], before).wait_recv()
            for j in range(1, X):
                remote(fw.at[m], ys.at[m + 2, pl.ds(j * rows, rows), :], ff_s.at[m], ff_r.at[m, j - 1], ends).wait_recv()

    def relay_sent(m):
        @pl.when(jnp.logical_and(pipe > 0, jnp.logical_not(is_edge)))
        def _():
            relay(m).wait_send()

        @pl.when(is_edge)
        def _():
            for c in relay_parts(m):
                c.wait_send()

        @pl.when(is_stop)
        def _():
            relay_on(m).wait_send()

    def grads(half, m):
        def body(i, carry):
            cols = pl.ds(pl.multiple_of(i * STEP, STEP), STEP)
            left = xg[m, :, cols] if half == 0 else ys[m, :, cols]
            right = qq[m, :, 0:lat] if half == 0 else kk[m]
            t = lax.dot_general(left, right, (((0,), (0,)), ((), ())), preferred_element_type=F32)
            if m == 0:
                acc[half, cols, :] = t
            else:
                acc[half, cols, :] += t
            return carry
        lax.fori_loop(0, quarter // STEP, body, 0)

    def far_block(k):
        return pl.ds(pl.multiple_of(lax.rem(z + k, Z) * block, 16), block)

    inner = jnp.logical_or(z == 1, z == 2)
    direct = [[remote(sb.at[half, k - 1], rb.at[half, k - 1], gr_s.at[half, k - 1], gr_r.at[half, k - 1], zpeer[k - 1])
               for k in range(1, Z)] for half in range(2)]
    ahead = [{k - 1: remote(sb.at[half, k - 1], via.at[half], via_s.at[half], via_r.at[half], zpeer[Z - k - 1])
              for k in (1, 3)} for half in range(2)]

    def blocks_start(half):
        @pl.when(z == 0)
        def _():
            for k in (3, 2, 1):
                sb[half, k - 1] = acc[half, far_block(k), :].astype(BF)
                (ahead if k == 3 else direct)[half][k - 1].start()

        @pl.when(z == 3)
        def _():
            for k in (1, 2, 3):
                sb[half, k - 1] = acc[half, far_block(k), :].astype(BF)
                (ahead if k == 1 else direct)[half][k - 1].start()

        @pl.when(inner)
        def _():
            for k in (1, 3):
                sb[half, k - 1] = acc[half, far_block(k), :].astype(BF)
                direct[half][k - 1].start()

    def blocks_pass(half):
        @pl.when(inner)
        def _():
            ahead[half][0].wait_recv()
            sb[half, 1] = (acc[half, far_block(2), :] + via[half].astype(F32)).astype(BF)
            direct[half][1].start()

    def blocks_end(half):
        near = pl.ds(pl.multiple_of(z * block, 16), block)
        total = acc[half, near, :].astype(BF).astype(F32)
        direct[half][1].wait_recv()
        total = total + rb[half, 1].astype(F32)

        @pl.when(z == 0)
        def _():
            direct[half][2].wait_recv()
            out_ref[half] = (total + rb[half, 2].astype(F32)).astype(BF)

        @pl.when(z == 3)
        def _():
            direct[half][0].wait_recv()
            out_ref[half] = (total + rb[half, 0].astype(F32)).astype(BF)

        @pl.when(inner)
        def _():
            direct[half][0].wait_recv()
            direct[half][2].wait_recv()
            out_ref[half] = (total + rb[half, 0].astype(F32) + rb[half, 2].astype(F32)).astype(BF)

    def blocks_sent(half):
        direct[half][1].wait_send()

        @pl.when(z == 0)
        def _():
            ahead[half][2].wait_send()
            direct[half][0].wait_send()

        @pl.when(z == 3)
        def _():
            ahead[half][0].wait_send()
            direct[half][2].wait_send()

        @pl.when(inner)
        def _():
            direct[half][0].wait_send()
            direct[half][2].wait_send()

    for i in (DX0, DY0):
        own_loads[i].wait()
    for c in w_loads:
        c.wait()
    arrive(down_x0)
    rc0 = part_c(0)
    arrive(down_y0)
    re0 = part_e(0)
    s0, gk0 = latent_k(0, rc0)
    gq0 = latent_q(0, s0, re0)
    arrive(gq0)
    input_grad(0)
    relay_start(0)

    inv[5] = inverse(UX1)
    inv[2] = inverse(DX1)
    arrive(gk0)
    grads(0, 0)
    grads(1, 0)
    relay_pass(0)
    own_loads[DX1].wait()
    arrive(down_x1)
    rc2 = part_c(2)
    s2, gk2 = latent_k(2, rc2)

    for c in up_x0 + up_y0:
        c.wait_send()
    up_x1 = send_up(UX1, xs.at[3])
    up_a1 = remote(inv.at[5], inv.at[3], a_s.at[1], a_r.at[1], mirror[0])
    up_a1.start()
    arrive(up_x0)
    rc1 = part_c(1)
    arrive(up_y0)
    re1 = part_e(1)
    up_a0.wait_recv()
    s1, gk1 = latent_k(1, rc1)
    gq1 = latent_q(1, s1, re1)
    arrive(gq1)
    input_grad(1)
    relay_start(1)

    relay_end(0)

    @pl.when(pipe == ranks - 1)
    def _():
        ys[2] = jnp.zeros((tokens, quarter), BF)
        ys[3] = jnp.zeros((tokens, quarter), BF)

    re2 = part_e(2)
    relay_pass(1)
    arrive(gk1)
    grads(0, 1)
    grads(1, 1)
    gq2 = latent_q(2, s2, re2)

    arrive(up_x1)
    rc3 = part_c(3)
    relay_end(1)
    re3 = part_e(3)
    up_a1.wait_recv()
    s3, gk3 = latent_k(3, rc3)
    arrive(gk2)
    grads(1, 2)
    arrive(gq2)
    grads(0, 2)
    gq3 = latent_q(3, s3, re3)
    arrive(gk3)
    grads(1, 3)
    blocks_start(1)
    arrive(gq3)
    grads(0, 3)
    blocks_pass(1)
    blocks_start(0)
    blocks_pass(0)
    blocks_end(1)
    blocks_end(0)
    blocks_sent(1)
    blocks_sent(0)

    for c in sent + up_x1 + [up_a0, up_a1]:
        c.wait_send()

    relay_sent(0)
    relay_sent(1)


def per_device(weights, gain_model, gain_latent, saved_down, saved_up, grad_start):
    _, _, width, lat = weights.shape
    rows = saved_down.shape[2]
    quarter = width // X
    block = quarter // Z
    tokens = X * rows
    dma = pltpu.SemaphoreType.DMA
    any_spec = pl.BlockSpec(memory_space=pl.ANY)
    vmem = pl.BlockSpec(memory_space=pltpu.VMEM)
    out = pl.pallas_call(
        kernel,
        out_shape=jax.ShapeDtypeStruct((2, block, lat), BF),
        in_specs=[any_spec] * 4 + [vmem] * 2,
        out_specs=vmem,
        scratch_shapes=[
            pltpu.VMEM((4, rows, width), BF),
            pltpu.VMEM((2, quarter, lat), BF),
            pltpu.VMEM((4, tokens, quarter), BF),
            pltpu.VMEM((4, tokens, quarter), BF),
            pltpu.VMEM((4, tokens, quarter), BF),
            pltpu.VMEM((2, tokens, quarter), BF),
            pltpu.VMEM((6, rows, 128), F32),
            pltpu.VMEM((4, 2, tokens, lat), F32),
            pltpu.VMEM((4, 2, tokens, lat), BF),
            pltpu.VMEM((4, 2, 3, rows, lat), BF),
            pltpu.VMEM((4, tokens, lat), BF),
            pltpu.VMEM((4, tokens, lat + 128), BF),
            pltpu.VMEM((2, quarter, lat), F32),
            pltpu.VMEM((2, 3, block, lat), BF),
            pltpu.VMEM((2, 3, block, lat), BF),
            pltpu.VMEM((2, block, lat), BF),
            pltpu.VMEM((2, rows, quarter), BF),
            dma((9,)),
            dma((6, 4)), dma((6, 4)),
            dma((2,)), dma((2,)),
            dma((4, 2, 3)), dma((4, 2, 3)),
            dma((4, 2, 3)), dma((4, 2, 3)),
            dma((2,)), dma((2,)),
            dma((2, 3)), dma((2, 3)),
            dma((2,)), dma((2,)),
            dma((2, 3)), dma((2,)), dma((2,)), dma((2, 3)),
        ],
        compiler_params=pltpu.CompilerParams(
            collective_id=0, has_side_effects=True, vmem_limit_bytes=56 << 20),
        name="relay_step",
    )(weights, saved_down, saved_up, grad_start, gain_model, gain_latent)
    return out[None]


def solution(mesh):
    placed = (
        P("pipe", None, None, None),
        P("pipe", None),
        P("pipe", None),
        P("pipe", None, "dp", None),
        P("pipe", None, "dp", None),
        P(None, "pipe", "dp", None),
    )
    return jax.shard_map(
        per_device,
        mesh=mesh,
        in_specs=placed,
        out_specs=P("pipe", None, "dp", None),
        check_vma=False,
    )
```

```python
import jax
import jax.numpy as jnp
from jax import lax
from jax.experimental import pallas as pl
from jax.experimental.pallas import tpu as pltpu
from jax.sharding import PartitionSpec as P

EPS = 1e-06
MESH = pl.DeviceIdType.MESH
BF = jnp.bfloat16
F32 = jnp.float32
X = 4
Z = 4
STEP = 1792
UX0, UY0, DX0, DY0, UX1, DX1 = range(6)


def kernel(w_hbm, sd_hbm, su_hbm, gs_hbm, gm_ref, gl_ref, out_ref,
           raw, w, xs, xg, ys, zr, inv, pf, pb, pr, kk, qq, acc, sb, rb, via, fw,
           lsem, in_s, in_r, a_s, a_r, rs_s, rs_r, ag_s, ag_r, rl_s, rl_r, gr_s, gr_r, via_s, via_r, fs_s, fs_r, ff_s, ff_r):
    pipe = lax.axis_index("pipe")
    dp = lax.axis_index("dp")
    ranks = lax.axis_size("pipe")
    x = dp // Z
    z = lax.rem(dp, Z)
    rows, width = raw.shape[1], raw.shape[2]
    quarter = width // X
    block = quarter // Z
    lat = w.shape[2]
    tokens = X * rows

    inputs = [su_hbm.at[0, 0], gs_hbm.at[1, 0], sd_hbm.at[0, 0], gs_hbm.at[0, 0], su_hbm.at[0, 1], sd_hbm.at[0, 1]]
    mine = pl.ds(pl.multiple_of(x * quarter, 128), quarter)
    here = pl.ds(pl.multiple_of(x * rows, rows), rows)
    raw_loads = {}
    for j, i in enumerate((UX0, DX0, UX1, DX1)):
        raw_loads[i] = (j, pltpu.make_async_copy(inputs[i], raw.at[j], lsem.at[j]))
    own_loads = {}
    for j, (i, dst) in enumerate(((DX0, xs.at[0]), (DY0, ys.at[0]), (DX1, xs.at[2]))):
        own_loads[i] = pltpu.make_async_copy(inputs[i].at[:, mine], dst.at[here], lsem.at[4 + j])
    w_loads = [pltpu.make_async_copy(w_hbm.at[0, half, mine, :], w.at[half], lsem.at[7 + half]) for half in range(2)]
    for c in [raw_loads[UX0][1], own_loads[DX0], w_loads[0], own_loads[DY0], w_loads[1],
              raw_loads[DX0][1], raw_loads[UX1][1], raw_loads[DX1][1], own_loads[DX1]]:
        c.start()

    mirror = [{"pipe": ranks - 1 - pipe, "dp": lax.rem(x + k, X) * Z + lax.rem(z + 2, Z)} for k in range(X)]
    xpeer = [{"pipe": pipe, "dp": lax.rem(x + k, X) * Z + z} for k in range(1, X)]
    zpeer = [{"pipe": pipe, "dp": x * Z + lax.rem(z + k, Z)} for k in range(1, Z)]
    before = {"pipe": lax.rem(pipe + ranks - 1, ranks), "dp": dp}
    after = {"pipe": lax.rem(pipe + 1, ranks), "dp": dp}
    barrier = pltpu.get_barrier_semaphore()
    greet = mirror + [before, after] + xpeer + zpeer
    for d in greet:
        pl.semaphore_signal(barrier, inc=1, device_id=d, device_id_type=MESH)

    edge = ranks // 2
    is_edge = pipe == edge
    is_end = pipe == edge - 1
    stops = [{"pipe": edge + 2 * j, "dp": dp} for j in range(1, X)]
    is_stop = jnp.logical_or(pipe == edge + 2, jnp.logical_or(pipe == edge + 4, pipe == edge + 6))
    ends = {"pipe": edge - 1, "dp": dp}

    @pl.when(jnp.logical_or(is_edge, is_end))
    def _():
        for d in stops:
            pl.semaphore_signal(barrier, inc=1, device_id=d, device_id_type=MESH)

    @pl.when(is_stop)
    def _():
        for d in ({"pipe": edge, "dp": dp}, ends):
            pl.semaphore_signal(barrier, inc=1, device_id=d, device_id_type=MESH)

    def remote(src, dst, ss, rs, dev):
        return pltpu.make_async_remote_copy(
            src_ref=src, dst_ref=dst, send_sem=ss, recv_sem=rs, device_id=dev, device_id_type=MESH)

    def inverse(i):
        j, load = raw_loads[i]
        load.wait()

        def body(n, ss):
            xf = raw[j, :, pl.ds(pl.multiple_of(n * 1024, 1024), 1024)].astype(F32)
            return ss + jnp.sum(xf * xf, axis=-1, keepdims=True)
        ss = lax.fori_loop(0, width // 1024, body, jnp.zeros((rows, 1), F32))
        return jnp.broadcast_to(lax.rsqrt(ss / width + EPS), (rows, 128))

    sent = []

    def cut(i, k):
        return inputs[i].at[:, pl.ds(pl.multiple_of(lax.rem(x + k, X) * quarter, 128), quarter)]

    def send_up(i, dst):
        cs = []
        for k in range(X):
            c = remote(cut(i, k), dst.at[here], in_s.at[i, k], in_r.at[i, k], mirror[k])
            c.start()
            cs.append(c)
        return cs

    def send_down(i, dst):
        cs = []
        for k in range(1, X):
            c = remote(cut(i, k), dst.at[here], in_s.at[i, k], in_r.at[i, k], xpeer[k - 1])
            c.start()
            cs.append(c)
        sent.extend(cs)
        return cs

    turn = jnp.logical_or(is_edge, is_end)

    @pl.when(turn)
    def _():
        pl.semaphore_wait(barrier, len(greet) + len(stops))

    @pl.when(is_stop)
    def _():
        pl.semaphore_wait(barrier, len(greet) + 2)

    @pl.when(jnp.logical_not(jnp.logical_or(turn, is_stop)))
    def _():
        pl.semaphore_wait(barrier, len(greet))

    up_x0 = send_up(UX0, xs.at[1])
    down_x0 = send_down(DX0, xs.at[0])
    down_y0 = send_down(DY0, ys.at[0])
    down_x1 = send_down(DX1, xs.at[2])
    inv[4] = inverse(UX0)
    up_a0 = remote(inv.at[4], inv.at[1], a_s.at[0], a_r.at[0], mirror[0])
    up_a0.start()
    inv[0] = inverse(DX0)
    h = gl_ref[...].astype(F32)

    def arrive(cs):
        for c in cs:
            c.wait_recv()

    def reduce_start(m, which, part):
        pf[m, which] = part
        pb[m, which] = part.astype(BF)
        cs = []
        for k in range(1, Z):
            far = pl.ds(pl.multiple_of(lax.rem(x + k, X) * rows, rows), rows)
            c = remote(pb.at[m, which, far, :], pr.at[m, which, k - 1],
                       rs_s.at[m, which, k - 1], rs_r.at[m, which, k - 1], xpeer[k - 1])
            c.start()
            cs.append(c)
        sent.extend(cs)
        return cs

    def reduce_end(m, which, cs):
        arrive(cs)
        total = pf[m, which, here, :]
        for k in range(1, Z):
            total = total + pr[m, which, k - 1].astype(F32)
        return total

    def gather_start(m, which, buf):
        cs = []
        for k in range(1, Z):
            c = remote(buf.at[m, here, :], buf.at[m, here, :],
                       ag_s.at[m, which, k - 1], ag_r.at[m, which, k - 1], xpeer[k - 1])
            c.start()
            cs.append(c)
        sent.extend(cs)
        return cs

    def gain(i):
        return gm_ref[:, pl.ds(pl.multiple_of(x * quarter + i * STEP, 128), STEP)].astype(F32)

    def part_c(m):
        def body(i, total):
            cols = pl.ds(pl.multiple_of(i * STEP, STEP), STEP)
            g = (xs[m, :, cols].astype(F32) * gain(i)).astype(BF)
            xg[m, :, cols] = g
            return total + jnp.dot(g, w[0, cols, :], preferred_element_type=F32)
        part = lax.fori_loop(0, quarter // STEP, body, jnp.zeros((tokens, lat), F32))
        return reduce_start(m, 0, part)

    def part_e(m):
        def body(i, total):
            cols = pl.ds(pl.multiple_of(i * STEP, STEP), STEP)
            return total + jnp.dot(ys[m, :, cols], w[1, cols, :], preferred_element_type=F32)
        part = lax.fori_loop(0, quarter // STEP, body, jnp.zeros((tokens, lat), F32))
        return reduce_start(m, 1, part)

    def latent_k(m, cs):
        total = reduce_end(m, 0, cs)
        a = inv[m, :, 0:1]
        c = total * a
        b = lax.rsqrt(jnp.mean(c * c, axis=-1, keepdims=True) + EPS)
        kk[m, here, :] = (c * b * h).astype(BF)
        return (a, b, c, total), gather_start(m, 0, kk)

    def latent_q(m, state, cs):
        a, b, c, total = state
        u = reduce_end(m, 1, cs) * h
        q = b * (u - c * b * b * jnp.mean(u * c, axis=-1, keepdims=True))
        aq = (a * q).astype(BF)
        t = a * a * jnp.sum(total * aq.astype(F32), axis=-1, keepdims=True) / width
        qq[m, here, 0:lat] = aq
        qq[m, here, lat:lat + 128] = jnp.broadcast_to(t, (rows, 128)).astype(BF)
        return gather_start(m, 1, qq)

    def input_grad(m):
        q = qq[m, :, 0:lat]
        t = qq[m, :, lat:lat + 1].astype(F32)
        def body(i, carry):
            cols = pl.ds(pl.multiple_of(i * STEP, STEP), STEP)
            v = lax.dot_general(q, w[0, cols, :], (((1,), (1,)), ((), ())), preferred_element_type=F32)
            zz = ys[m, :, cols].astype(F32) + v * gain(i) - xs[m, :, cols].astype(F32) * t
            zr[m, :, cols] = zz.astype(BF)
            return carry
        lax.fori_loop(0, quarter // STEP, body, 0)

    def relay(m):
        return remote(zr.at[m], ys.at[m + 2], rl_s.at[m], rl_r.at[m], before)

    def relay_parts(m):
        first = pl.ds(0, rows)
        cs = [remote(zr.at[m, first, :], ys.at[m + 2, first, :], rl_s.at[m], rl_r.at[m], before)]
        for j in range(1, X):
            cs.append(remote(zr.at[m, pl.ds(j * rows, rows), :], fw.at[m], fs_s.at[m, j - 1], fs_r.at[m], stops[j - 1]))
        return cs

    def relay_on(m):
        j = (pipe - edge) // 2
        there = pl.ds(pl.multiple_of(j * rows, rows), rows)
        return remote(fw.at[m], ys.at[m + 2, there, :], ff_s.at[m], ff_r.at[m, j - 1], ends)

    def relay_start(m):
        @pl.when(jnp.logical_and(pipe > 0, jnp.logical_not(is_edge)))
        def _():
            relay(m).start()

        @pl.when(is_edge)
        def _():
            for c in relay_parts(m):
                c.start()

    def relay_pass(m):
        @pl.when(is_stop)
        def _():
            remote(zr.at[m, pl.ds(0, rows), :], fw.at[m], fs_s.at[m, 0], fs_r.at[m], stops[0]).wait_recv()
            relay_on(m).start()

    def relay_end(m):
        @pl.when(jnp.logical_and(pipe < ranks - 1, jnp.logical_not(is_end)))
        def _():
            relay(m).wait_recv()

        @pl.when(is_end)
        def _():
            first = pl.ds(0, rows)
            remote(zr.at[m, first, :], ys.at[m + 2, first, :], rl_s.at[m], rl_r.at[m], before).wait_recv()
            for j in range(1, X):
                remote(fw.at[m], ys.at[m + 2, pl.ds(j * rows, rows), :], ff_s.at[m], ff_r.at[m, j - 1], ends).wait_recv()

    def relay_sent(m):
        @pl.when(jnp.logical_and(pipe > 0, jnp.logical_not(is_edge)))
        def _():
            relay(m).wait_send()

        @pl.when(is_edge)
        def _():
            for c in relay_parts(m):
                c.wait_send()

        @pl.when(is_stop)
        def _():
            relay_on(m).wait_send()

    def grads(half, m):
        def body(i, carry):
            cols = pl.ds(pl.multiple_of(i * 896, 896), 896)
            left = xg[m, :, cols] if half == 0 else ys[m, :, cols]
            right = qq[m, :, 0:lat] if half == 0 else kk[m]
            t = lax.dot_general(left, right, (((0,), (0,)), ((), ())), preferred_element_type=F32)
            if m == 0:
                acc[half, cols, :] = t
            else:
                acc[half, cols, :] += t
            return carry
        lax.fori_loop(0, quarter // 896, body, 0)

    def far_block(k):
        return pl.ds(pl.multiple_of(lax.rem(z + k, Z) * block, 16), block)

    inner = jnp.logical_or(z == 1, z == 2)
    direct = [[remote(sb.at[half, k - 1], rb.at[half, k - 1], gr_s.at[half, k - 1], gr_r.at[half, k - 1], zpeer[k - 1])
               for k in range(1, Z)] for half in range(2)]
    ahead = [{k - 1: remote(sb.at[half, k - 1], via.at[half], via_s.at[half], via_r.at[half], zpeer[Z - k - 1])
              for k in (1, 3)} for half in range(2)]

    def blocks_start(half):
        @pl.when(z == 0)
        def _():
            for k in (3, 2, 1):
                sb[half, k - 1] = acc[half, far_block(k), :].astype(BF)
                (ahead if k == 3 else direct)[half][k - 1].start()

        @pl.when(z == 3)
        def _():
            for k in (1, 2, 3):
                sb[half, k - 1] = acc[half, far_block(k), :].astype(BF)
                (ahead if k == 1 else direct)[half][k - 1].start()

        @pl.when(inner)
        def _():
            for k in (1, 3):
                sb[half, k - 1] = acc[half, far_block(k), :].astype(BF)
                direct[half][k - 1].start()

    def blocks_pass(half):
        @pl.when(inner)
        def _():
            ahead[half][0].wait_recv()
            sb[half, 1] = (acc[half, far_block(2), :] + via[half].astype(F32)).astype(BF)
            direct[half][1].start()

    def blocks_end(half):
        near = pl.ds(pl.multiple_of(z * block, 16), block)
        total = acc[half, near, :].astype(BF).astype(F32)
        direct[half][1].wait_recv()
        total = total + rb[half, 1].astype(F32)

        @pl.when(z == 0)
        def _():
            direct[half][2].wait_recv()
            out_ref[half] = (total + rb[half, 2].astype(F32)).astype(BF)

        @pl.when(z == 3)
        def _():
            direct[half][0].wait_recv()
            out_ref[half] = (total + rb[half, 0].astype(F32)).astype(BF)

        @pl.when(inner)
        def _():
            direct[half][0].wait_recv()
            direct[half][2].wait_recv()
            out_ref[half] = (total + rb[half, 0].astype(F32) + rb[half, 2].astype(F32)).astype(BF)

    def blocks_sent(half):
        direct[half][1].wait_send()

        @pl.when(z == 0)
        def _():
            ahead[half][2].wait_send()
            direct[half][0].wait_send()

        @pl.when(z == 3)
        def _():
            ahead[half][0].wait_send()
            direct[half][2].wait_send()

        @pl.when(inner)
        def _():
            direct[half][0].wait_send()
            direct[half][2].wait_send()

    for i in (DX0, DY0):
        own_loads[i].wait()
    for c in w_loads:
        c.wait()
    arrive(down_x0)
    rc0 = part_c(0)
    arrive(down_y0)
    re0 = part_e(0)
    up_y0 = send_up(UY0, ys.at[1])
    s0, gk0 = latent_k(0, rc0)
    gq0 = latent_q(0, s0, re0)
    arrive(gq0)
    input_grad(0)
    relay_start(0)

    inv[5] = inverse(UX1)
    inv[2] = inverse(DX1)
    arrive(gk0)
    grads(0, 0)
    grads(1, 0)
    relay_pass(0)
    own_loads[DX1].wait()
    arrive(down_x1)
    rc2 = part_c(2)
    s2, gk2 = latent_k(2, rc2)

    arrive(up_x0)
    rc1 = part_c(1)
    up_a0.wait_recv()
    s1, gk1 = latent_k(1, rc1)
    for c in up_x0 + up_y0:
        c.wait_send()
    up_x1 = send_up(UX1, xs.at[3])
    up_a1 = remote(inv.at[5], inv.at[3], a_s.at[1], a_r.at[1], mirror[0])
    up_a1.start()
    arrive(up_y0)
    re1 = part_e(1)
    gq1 = latent_q(1, s1, re1)
    arrive(gq1)
    input_grad(1)
    relay_start(1)

    relay_end(0)

    @pl.when(pipe == ranks - 1)
    def _():
        ys[2] = jnp.zeros((tokens, quarter), BF)
        ys[3] = jnp.zeros((tokens, quarter), BF)

    re2 = part_e(2)
    relay_pass(1)
    arrive(gk1)
    grads(0, 1)
    grads(1, 1)
    gq2 = latent_q(2, s2, re2)

    arrive(up_x1)
    rc3 = part_c(3)
    relay_end(1)
    re3 = part_e(3)
    up_a1.wait_recv()
    s3, gk3 = latent_k(3, rc3)
    arrive(gk2)
    grads(1, 2)
    arrive(gq2)
    grads(0, 2)
    gq3 = latent_q(3, s3, re3)
    arrive(gk3)
    grads(1, 3)
    blocks_start(1)
    arrive(gq3)
    grads(0, 3)
    blocks_pass(1)
    blocks_start(0)
    blocks_pass(0)
    blocks_end(1)
    blocks_end(0)
    blocks_sent(1)
    blocks_sent(0)

    for c in sent + up_x1 + [up_a0, up_a1]:
        c.wait_send()

    relay_sent(0)
    relay_sent(1)


def per_device(weights, gain_model, gain_latent, saved_down, saved_up, grad_start):
    _, _, width, lat = weights.shape
    rows = saved_down.shape[2]
    quarter = width // X
    block = quarter // Z
    tokens = X * rows
    dma = pltpu.SemaphoreType.DMA
    any_spec = pl.BlockSpec(memory_space=pl.ANY)
    vmem = pl.BlockSpec(memory_space=pltpu.VMEM)
    out = pl.pallas_call(
        kernel,
        out_shape=jax.ShapeDtypeStruct((2, block, lat), BF),
        in_specs=[any_spec] * 4 + [vmem] * 2,
        out_specs=vmem,
        scratch_shapes=[
            pltpu.VMEM((4, rows, width), BF),
            pltpu.VMEM((2, quarter, lat), BF),
            pltpu.VMEM((4, tokens, quarter), BF),
            pltpu.VMEM((4, tokens, quarter), BF),
            pltpu.VMEM((4, tokens, quarter), BF),
            pltpu.VMEM((2, tokens, quarter), BF),
            pltpu.VMEM((6, rows, 128), F32),
            pltpu.VMEM((4, 2, tokens, lat), F32),
            pltpu.VMEM((4, 2, tokens, lat), BF),
            pltpu.VMEM((4, 2, 3, rows, lat), BF),
            pltpu.VMEM((4, tokens, lat), BF),
            pltpu.VMEM((4, tokens, lat + 128), BF),
            pltpu.VMEM((2, quarter, lat), F32),
            pltpu.VMEM((2, 3, block, lat), BF),
            pltpu.VMEM((2, 3, block, lat), BF),
            pltpu.VMEM((2, block, lat), BF),
            pltpu.VMEM((2, rows, quarter), BF),
            dma((9,)),
            dma((6, 4)), dma((6, 4)),
            dma((2,)), dma((2,)),
            dma((4, 2, 3)), dma((4, 2, 3)),
            dma((4, 2, 3)), dma((4, 2, 3)),
            dma((2,)), dma((2,)),
            dma((2, 3)), dma((2, 3)),
            dma((2,)), dma((2,)),
            dma((2, 3)), dma((2,)), dma((2,)), dma((2, 3)),
        ],
        compiler_params=pltpu.CompilerParams(
            collective_id=0, has_side_effects=True, vmem_limit_bytes=56 << 20),
        name="relay_step",
    )(weights, saved_down, saved_up, grad_start, gain_model, gain_latent)
    return out[None]


def solution(mesh):
    placed = (
        P("pipe", None, None, None),
        P("pipe", None),
        P("pipe", None),
        P("pipe", None, "dp", None),
        P("pipe", None, "dp", None),
        P(None, "pipe", "dp", None),
    )
    return jax.shard_map(
        per_device,
        mesh=mesh,
        in_specs=placed,
        out_specs=P("pipe", None, "dp", None),
        check_vma=False,
    )
```

```python
import jax
import jax.numpy as jnp
from jax import lax
from jax.experimental import pallas as pl
from jax.experimental.pallas import tpu as pltpu
from jax.sharding import PartitionSpec as P

EPS = 1e-06
MESH = pl.DeviceIdType.MESH
BF = jnp.bfloat16
F32 = jnp.float32
X = 4
Z = 4
STEP = 1792
UX0, UY0, DX0, DY0, UX1, DX1 = range(6)


def kernel(w_hbm, sd_hbm, su_hbm, gs_hbm, gm_ref, gl_ref, out_ref,
           raw, w, xs, xg, ys, zr, inv, pf, pb, pr, kk, qq, acc, sb, rb, via, fw,
           lsem, in_s, in_r, a_s, a_r, rs_s, rs_r, ag_s, ag_r, rl_s, rl_r, gr_s, gr_r, via_s, via_r, fs_s, fs_r, ff_s, ff_r):
    pipe = lax.axis_index("pipe")
    dp = lax.axis_index("dp")
    ranks = lax.axis_size("pipe")
    x = dp // Z
    z = lax.rem(dp, Z)
    rows, width = raw.shape[1], raw.shape[2]
    quarter = width // X
    block = quarter // Z
    lat = w.shape[2]
    tokens = X * rows

    inputs = [su_hbm.at[0, 0], gs_hbm.at[1, 0], sd_hbm.at[0, 0], gs_hbm.at[0, 0], su_hbm.at[0, 1], sd_hbm.at[0, 1]]
    mine = pl.ds(pl.multiple_of(x * quarter, 128), quarter)
    here = pl.ds(pl.multiple_of(x * rows, rows), rows)
    raw_loads = {}
    for j, i in enumerate((UX0, DX0, UX1, DX1)):
        raw_loads[i] = (j, pltpu.make_async_copy(inputs[i], raw.at[j], lsem.at[j]))
    own_loads = {}
    for j, (i, dst) in enumerate(((DX0, xs.at[0]), (DY0, ys.at[0]), (DX1, xs.at[2]))):
        own_loads[i] = pltpu.make_async_copy(inputs[i].at[:, mine], dst.at[here], lsem.at[4 + j])
    w_loads = [pltpu.make_async_copy(w_hbm.at[0, half, mine, :], w.at[half], lsem.at[7 + half]) for half in range(2)]
    mirror = [{"pipe": ranks - 1 - pipe, "dp": lax.rem(x + k, X) * Z + lax.rem(z + 2, Z)} for k in range(X)]
    xpeer = [{"pipe": pipe, "dp": lax.rem(x + k, X) * Z + z} for k in range(1, X)]
    zpeer = [{"pipe": pipe, "dp": x * Z + lax.rem(z + k, Z)} for k in range(1, Z)]
    before = {"pipe": lax.rem(pipe + ranks - 1, ranks), "dp": dp}
    after = {"pipe": lax.rem(pipe + 1, ranks), "dp": dp}
    barrier = pltpu.get_barrier_semaphore()
    greet = mirror + [before, after] + xpeer + zpeer
    for d in greet:
        pl.semaphore_signal(barrier, inc=1, device_id=d, device_id_type=MESH)

    edge = ranks // 2
    is_edge = pipe == edge
    is_end = pipe == edge - 1
    stops = [{"pipe": edge + 2 * j, "dp": dp} for j in range(1, X)]
    is_stop = jnp.logical_or(pipe == edge + 2, jnp.logical_or(pipe == edge + 4, pipe == edge + 6))
    ends = {"pipe": edge - 1, "dp": dp}

    @pl.when(jnp.logical_or(is_edge, is_end))
    def _():
        for d in stops:
            pl.semaphore_signal(barrier, inc=1, device_id=d, device_id_type=MESH)

    @pl.when(is_stop)
    def _():
        for d in ({"pipe": edge, "dp": dp}, ends):
            pl.semaphore_signal(barrier, inc=1, device_id=d, device_id_type=MESH)

    for c in [raw_loads[UX0][1], own_loads[DX0], w_loads[0], own_loads[DY0], w_loads[1],
              raw_loads[DX0][1], raw_loads[UX1][1], raw_loads[DX1][1], own_loads[DX1]]:
        c.start()

    def remote(src, dst, ss, rs, dev):
        return pltpu.make_async_remote_copy(
            src_ref=src, dst_ref=dst, send_sem=ss, recv_sem=rs, device_id=dev, device_id_type=MESH)

    def inverse(i):
        j, load = raw_loads[i]
        load.wait()

        def body(n, ss):
            xf = raw[j, :, pl.ds(pl.multiple_of(n * 1024, 1024), 1024)].astype(F32)
            return ss + jnp.sum(xf * xf, axis=-1, keepdims=True)
        ss = lax.fori_loop(0, width // 1024, body, jnp.zeros((rows, 1), F32))
        return jnp.broadcast_to(lax.rsqrt(ss / width + EPS), (rows, 128))

    sent = []

    def cut(i, k):
        return inputs[i].at[:, pl.ds(pl.multiple_of(lax.rem(x + k, X) * quarter, 128), quarter)]

    def send_up(i, dst):
        cs = []
        for k in range(X):
            c = remote(cut(i, k), dst.at[here], in_s.at[i, k], in_r.at[i, k], mirror[k])
            c.start()
            cs.append(c)
        return cs

    def send_down(i, dst):
        cs = []
        for k in range(1, X):
            c = remote(cut(i, k), dst.at[here], in_s.at[i, k], in_r.at[i, k], xpeer[k - 1])
            c.start()
            cs.append(c)
        sent.extend(cs)
        return cs

    turn = jnp.logical_or(is_edge, is_end)

    @pl.when(turn)
    def _():
        pl.semaphore_wait(barrier, len(greet) + len(stops))

    @pl.when(is_stop)
    def _():
        pl.semaphore_wait(barrier, len(greet) + 2)

    @pl.when(jnp.logical_not(jnp.logical_or(turn, is_stop)))
    def _():
        pl.semaphore_wait(barrier, len(greet))

    up_x0 = send_up(UX0, xs.at[1])
    down_x0 = send_down(DX0, xs.at[0])
    down_y0 = send_down(DY0, ys.at[0])
    down_x1 = send_down(DX1, xs.at[2])
    inv[4] = inverse(UX0)
    up_a0 = remote(inv.at[4], inv.at[1], a_s.at[0], a_r.at[0], mirror[0])
    up_a0.start()
    inv[0] = inverse(DX0)
    h = gl_ref[...].astype(F32)

    def arrive(cs):
        for c in cs:
            c.wait_recv()

    def reduce_start(m, which, part):
        pf[m, which] = part
        pb[m, which] = part.astype(BF)
        cs = []
        for k in range(1, Z):
            far = pl.ds(pl.multiple_of(lax.rem(x + k, X) * rows, rows), rows)
            c = remote(pb.at[m, which, far, :], pr.at[m, which, k - 1],
                       rs_s.at[m, which, k - 1], rs_r.at[m, which, k - 1], xpeer[k - 1])
            c.start()
            cs.append(c)
        sent.extend(cs)
        return cs

    def reduce_end(m, which, cs):
        arrive(cs)
        total = pf[m, which, here, :]
        for k in range(1, Z):
            total = total + pr[m, which, k - 1].astype(F32)
        return total

    def gather_start(m, which, buf):
        cs = []
        for k in range(1, Z):
            c = remote(buf.at[m, here, :], buf.at[m, here, :],
                       ag_s.at[m, which, k - 1], ag_r.at[m, which, k - 1], xpeer[k - 1])
            c.start()
            cs.append(c)
        sent.extend(cs)
        return cs

    def gain(i):
        return gm_ref[:, pl.ds(pl.multiple_of(x * quarter + i * STEP, 128), STEP)].astype(F32)

    def part_c(m):
        def body(i, total):
            cols = pl.ds(pl.multiple_of(i * STEP, STEP), STEP)
            g = (xs[m, :, cols].astype(F32) * gain(i)).astype(BF)
            xg[m, :, cols] = g
            return total + jnp.dot(g, w[0, cols, :], preferred_element_type=F32)
        part = lax.fori_loop(0, quarter // STEP, body, jnp.zeros((tokens, lat), F32))
        return reduce_start(m, 0, part)

    def part_e(m):
        def body(i, total):
            cols = pl.ds(pl.multiple_of(i * STEP, STEP), STEP)
            return total + jnp.dot(ys[m, :, cols], w[1, cols, :], preferred_element_type=F32)
        part = lax.fori_loop(0, quarter // STEP, body, jnp.zeros((tokens, lat), F32))
        return reduce_start(m, 1, part)

    def latent_k(m, cs):
        total = reduce_end(m, 0, cs)
        a = inv[m, :, 0:1]
        c = total * a
        b = lax.rsqrt(jnp.mean(c * c, axis=-1, keepdims=True) + EPS)
        kk[m, here, :] = (c * b * h).astype(BF)
        return (a, b, c, total), gather_start(m, 0, kk)

    def latent_q(m, state, cs):
        a, b, c, total = state
        u = reduce_end(m, 1, cs) * h
        q = b * (u - c * b * b * jnp.mean(u * c, axis=-1, keepdims=True))
        aq = (a * q).astype(BF)
        t = a * a * jnp.sum(total * aq.astype(F32), axis=-1, keepdims=True) / width
        qq[m, here, 0:lat] = aq
        qq[m, here, lat:lat + 128] = jnp.broadcast_to(t, (rows, 128)).astype(BF)
        return gather_start(m, 1, qq)

    def input_grad(m):
        q = qq[m, :, 0:lat]
        t = qq[m, :, lat:lat + 1].astype(F32)
        def body(i, carry):
            cols = pl.ds(pl.multiple_of(i * STEP, STEP), STEP)
            v = lax.dot_general(q, w[0, cols, :], (((1,), (1,)), ((), ())), preferred_element_type=F32)
            zz = ys[m, :, cols].astype(F32) + v * gain(i) - xs[m, :, cols].astype(F32) * t
            zr[m, :, cols] = zz.astype(BF)
            return carry
        lax.fori_loop(0, quarter // STEP, body, 0)

    def relay(m):
        return remote(zr.at[m], ys.at[m + 2], rl_s.at[m], rl_r.at[m], before)

    def relay_parts(m):
        first = pl.ds(0, rows)
        cs = [remote(zr.at[m, first, :], ys.at[m + 2, first, :], rl_s.at[m], rl_r.at[m], before)]
        for j in range(1, X):
            cs.append(remote(zr.at[m, pl.ds(j * rows, rows), :], fw.at[m], fs_s.at[m, j - 1], fs_r.at[m], stops[j - 1]))
        return cs

    def relay_on(m):
        j = (pipe - edge) // 2
        there = pl.ds(pl.multiple_of(j * rows, rows), rows)
        return remote(fw.at[m], ys.at[m + 2, there, :], ff_s.at[m], ff_r.at[m, j - 1], ends)

    def relay_start(m):
        @pl.when(jnp.logical_and(pipe > 0, jnp.logical_not(is_edge)))
        def _():
            relay(m).start()

        @pl.when(is_edge)
        def _():
            for c in relay_parts(m):
                c.start()

    def relay_pass(m):
        @pl.when(is_stop)
        def _():
            remote(zr.at[m, pl.ds(0, rows), :], fw.at[m], fs_s.at[m, 0], fs_r.at[m], stops[0]).wait_recv()
            relay_on(m).start()

    def relay_end(m):
        @pl.when(jnp.logical_and(pipe < ranks - 1, jnp.logical_not(is_end)))
        def _():
            relay(m).wait_recv()

        @pl.when(is_end)
        def _():
            first = pl.ds(0, rows)
            remote(zr.at[m, first, :], ys.at[m + 2, first, :], rl_s.at[m], rl_r.at[m], before).wait_recv()
            for j in range(1, X):
                remote(fw.at[m], ys.at[m + 2, pl.ds(j * rows, rows), :], ff_s.at[m], ff_r.at[m, j - 1], ends).wait_recv()

    def relay_sent(m):
        @pl.when(jnp.logical_and(pipe > 0, jnp.logical_not(is_edge)))
        def _():
            relay(m).wait_send()

        @pl.when(is_edge)
        def _():
            for c in relay_parts(m):
                c.wait_send()

        @pl.when(is_stop)
        def _():
            relay_on(m).wait_send()

    def grads(half, m):
        def body(i, carry):
            cols = pl.ds(pl.multiple_of(i * 896, 896), 896)
            left = xg[m, :, cols] if half == 0 else ys[m, :, cols]
            right = qq[m, :, 0:lat] if half == 0 else kk[m]
            t = lax.dot_general(left, right, (((0,), (0,)), ((), ())), preferred_element_type=F32)
            if m == 0:
                acc[half, cols, :] = t
            else:
                acc[half, cols, :] += t
            return carry
        lax.fori_loop(0, quarter // 896, body, 0)

    def far_block(k):
        return pl.ds(pl.multiple_of(lax.rem(z + k, Z) * block, 16), block)

    inner = jnp.logical_or(z == 1, z == 2)
    direct = [[remote(sb.at[half, k - 1], rb.at[half, k - 1], gr_s.at[half, k - 1], gr_r.at[half, k - 1], zpeer[k - 1])
               for k in range(1, Z)] for half in range(2)]
    ahead = [{k - 1: remote(sb.at[half, k - 1], via.at[half], via_s.at[half], via_r.at[half], zpeer[Z - k - 1])
              for k in (1, 3)} for half in range(2)]

    def blocks_start(half):
        @pl.when(z == 0)
        def _():
            for k in (3, 2, 1):
                sb[half, k - 1] = acc[half, far_block(k), :].astype(BF)
                (ahead if k == 3 else direct)[half][k - 1].start()

        @pl.when(z == 3)
        def _():
            for k in (1, 2, 3):
                sb[half, k - 1] = acc[half, far_block(k), :].astype(BF)
                (ahead if k == 1 else direct)[half][k - 1].start()

        @pl.when(inner)
        def _():
            for k in (1, 3):
                sb[half, k - 1] = acc[half, far_block(k), :].astype(BF)
                direct[half][k - 1].start()

    def blocks_pass(half):
        @pl.when(inner)
        def _():
            ahead[half][0].wait_recv()
            sb[half, 1] = (acc[half, far_block(2), :] + via[half].astype(F32)).astype(BF)
            direct[half][1].start()

    def blocks_end(half):
        near = pl.ds(pl.multiple_of(z * block, 16), block)
        total = acc[half, near, :].astype(BF).astype(F32)
        direct[half][1].wait_recv()
        total = total + rb[half, 1].astype(F32)

        @pl.when(z == 0)
        def _():
            direct[half][2].wait_recv()
            out_ref[half] = (total + rb[half, 2].astype(F32)).astype(BF)

        @pl.when(z == 3)
        def _():
            direct[half][0].wait_recv()
            out_ref[half] = (total + rb[half, 0].astype(F32)).astype(BF)

        @pl.when(inner)
        def _():
            direct[half][0].wait_recv()
            direct[half][2].wait_recv()
            out_ref[half] = (total + rb[half, 0].astype(F32) + rb[half, 2].astype(F32)).astype(BF)

    def blocks_sent(half):
        direct[half][1].wait_send()

        @pl.when(z == 0)
        def _():
            ahead[half][2].wait_send()
            direct[half][0].wait_send()

        @pl.when(z == 3)
        def _():
            ahead[half][0].wait_send()
            direct[half][2].wait_send()

        @pl.when(inner)
        def _():
            direct[half][0].wait_send()
            direct[half][2].wait_send()

    for i in (DX0, DY0):
        own_loads[i].wait()
    for c in w_loads:
        c.wait()
    arrive(down_x0)
    rc0 = part_c(0)
    arrive(down_y0)
    re0 = part_e(0)
    up_y0 = send_up(UY0, ys.at[1])
    s0, gk0 = latent_k(0, rc0)
    gq0 = latent_q(0, s0, re0)
    arrive(gq0)
    input_grad(0)
    relay_start(0)

    inv[5] = inverse(UX1)
    inv[2] = inverse(DX1)
    arrive(gk0)
    grads(0, 0)
    grads(1, 0)
    relay_pass(0)
    own_loads[DX1].wait()
    arrive(down_x1)
    rc2 = part_c(2)
    s2, gk2 = latent_k(2, rc2)

    arrive(up_x0)
    rc1 = part_c(1)
    up_a0.wait_recv()
    s1, gk1 = latent_k(1, rc1)
    for c in up_x0 + up_y0:
        c.wait_send()
    up_x1 = send_up(UX1, xs.at[3])
    up_a1 = remote(inv.at[5], inv.at[3], a_s.at[1], a_r.at[1], mirror[0])
    up_a1.start()
    arrive(up_y0)
    re1 = part_e(1)
    gq1 = latent_q(1, s1, re1)
    arrive(gq1)
    input_grad(1)
    relay_start(1)

    relay_end(0)

    @pl.when(pipe == ranks - 1)
    def _():
        ys[2] = jnp.zeros((tokens, quarter), BF)
        ys[3] = jnp.zeros((tokens, quarter), BF)

    relay_pass(1)
    re2 = part_e(2)
    arrive(gk1)
    grads(0, 1)
    grads(1, 1)
    gq2 = latent_q(2, s2, re2)

    arrive(up_x1)
    rc3 = part_c(3)
    relay_end(1)
    re3 = part_e(3)
    up_a1.wait_recv()
    s3, gk3 = latent_k(3, rc3)
    arrive(gk2)
    grads(1, 2)
    arrive(gq2)
    grads(0, 2)
    gq3 = latent_q(3, s3, re3)
    arrive(gk3)
    grads(1, 3)
    blocks_start(1)
    arrive(gq3)
    grads(0, 3)
    blocks_pass(1)
    blocks_start(0)
    blocks_pass(0)
    blocks_end(1)
    blocks_end(0)
    blocks_sent(1)
    blocks_sent(0)

    for c in sent + up_x1 + [up_a0, up_a1]:
        c.wait_send()

    relay_sent(0)
    relay_sent(1)


def per_device(weights, gain_model, gain_latent, saved_down, saved_up, grad_start):
    _, _, width, lat = weights.shape
    rows = saved_down.shape[2]
    quarter = width // X
    block = quarter // Z
    tokens = X * rows
    dma = pltpu.SemaphoreType.DMA
    any_spec = pl.BlockSpec(memory_space=pl.ANY)
    vmem = pl.BlockSpec(memory_space=pltpu.VMEM)
    out = pl.pallas_call(
        kernel,
        out_shape=jax.ShapeDtypeStruct((2, block, lat), BF),
        in_specs=[any_spec] * 4 + [vmem] * 2,
        out_specs=vmem,
        scratch_shapes=[
            pltpu.VMEM((4, rows, width), BF),
            pltpu.VMEM((2, quarter, lat), BF),
            pltpu.VMEM((4, tokens, quarter), BF),
            pltpu.VMEM((4, tokens, quarter), BF),
            pltpu.VMEM((4, tokens, quarter), BF),
            pltpu.VMEM((2, tokens, quarter), BF),
            pltpu.VMEM((6, rows, 128), F32),
            pltpu.VMEM((4, 2, tokens, lat), F32),
            pltpu.VMEM((4, 2, tokens, lat), BF),
            pltpu.VMEM((4, 2, 3, rows, lat), BF),
            pltpu.VMEM((4, tokens, lat), BF),
            pltpu.VMEM((4, tokens, lat + 128), BF),
            pltpu.VMEM((2, quarter, lat), F32),
            pltpu.VMEM((2, 3, block, lat), BF),
            pltpu.VMEM((2, 3, block, lat), BF),
            pltpu.VMEM((2, block, lat), BF),
            pltpu.VMEM((2, rows, quarter), BF),
            dma((9,)),
            dma((6, 4)), dma((6, 4)),
            dma((2,)), dma((2,)),
            dma((4, 2, 3)), dma((4, 2, 3)),
            dma((4, 2, 3)), dma((4, 2, 3)),
            dma((2,)), dma((2,)),
            dma((2, 3)), dma((2, 3)),
            dma((2,)), dma((2,)),
            dma((2, 3)), dma((2,)), dma((2,)), dma((2, 3)),
        ],
        compiler_params=pltpu.CompilerParams(
            collective_id=0, has_side_effects=True, vmem_limit_bytes=56 << 20),
        name="relay_step",
    )(weights, saved_down, saved_up, grad_start, gain_model, gain_latent)
    return out[None]


def solution(mesh):
    placed = (
        P("pipe", None, None, None),
        P("pipe", None),
        P("pipe", None),
        P("pipe", None, "dp", None),
        P("pipe", None, "dp", None),
        P(None, "pipe", "dp", None),
    )
    return jax.shard_map(
        per_device,
        mesh=mesh,
        in_specs=placed,
        out_specs=P("pipe", None, "dp", None),
        check_vma=False,
    )
```
